32 devices in a mesh: parts: 2 (over y), space: 8 (over z, x), dp: 2 (over core).
Axes of the slice: x: 2, y: 2, z: 4, core: 2. Of those that a mesh axis runs over, the one named last changes fastest.
Arguments:
- volume: bfloat16 [4, 128, 32, 128, 128], P(('parts', 'dp'), 'space'), parts along dimension 0, may hold values from -6 to 6
- cotangent: bfloat16 [4, 128, 32, 128, 128], P(('parts', 'dp'), 'space'), parts along dimension 0, may hold values from -6 to 6
- spectral_weight: bfloat16 [2, 32, 512, 32, 32], P(None, None, 'space')
- pointwise_weight: bfloat16 [32, 32], replicated, may hold values from -1 to 1
- gain_table: bfloat16 [4096, 32], replicated, may hold values from 0.099609375 to 1.8984375
- bias_index: int32 [4], P(('parts', 'dp')), parts along dimension 0, may hold values from 0 to 4095
Outputs:
- input_grad: bfloat16 [4, 128, 32, 128, 128], P(('parts', 'dp'), 'space'), parts along dimension 0
- spectral_grad: float32 [4, 32, 512, 32, 32], P('parts', None, 'space', None, 'dp'), parts along dimension 0
The draws below stay inside these ranges and needn't reach their ends.
There are 2 independent parts, one for each index of `parts`. The reference program is written for one: setup_inputs(seed, part) draws one part's arguments, and reference() takes and returns one part's arrays. A program takes and returns all parts, laid end to end along the dimension named above; an argument that names none is the same for every part. Nothing has to cross between parts.
All inputs are finite; a program needn't handle non-finite values.
Results may differ from the reference program's by a relative error of at most 0.01.
Values may be sent and summed in bfloat16 or wider, within the bound.
No kernel may reach another device: no remote copies, remote signals or barrier semaphores. Data moves between devices by JAX's collectives and lax.ppermute only.
A program may use at most 256 MiB of HBM per device.

```python
import math
import jax
import jax.numpy as jnp
from jax import lax

C = 32
M = 16
NX = 128
NY = 128
NZ = 128
BIAS = 4096
S = 2


def draw_spectral_weight(key, part):
    spread = math.sqrt(NX * NY * NZ / (4.0 * M * M * M * C))
    full_shape = (2, 2 * M, 2 * M * M, C, C)
    values_out = jax.random.normal(key, full_shape, jnp.float32) * spread
    return values_out.astype(jnp.bfloat16)


def block_scale(stream_key, extent, split, low, largest):
    def one(dim, blocks):
        draws = jax.random.uniform(jax.random.fold_in(jax.random.fold_in(stream_key, 6), dim), (blocks,), jnp.float32, low / len(split), largest / len(split))
        return jnp.repeat(jnp.exp(draws), extent[dim] // blocks).reshape((-1,) + (1,) * (len(extent) - dim - 1))

    gain = one(*split[0])
    for cut in split[1:]:
        gain = gain * one(*cut)
    return gain


def centred(own_key, dims, width, bound, pieces=(), kind=jnp.bfloat16):
    values = jax.random.normal(own_key, dims, jnp.float32) * width
    if len(pieces) > 0:
        values = block_scale(own_key, dims, pieces, -0.22, 0.18) * values
    return jnp.clip(values, min=-bound, max=bound).astype(kind)


def setup_inputs(seed: int = 0, part: int = 0) -> dict:
    arg_keys = jax.random.split(jax.random.key(seed), 7)
    own_keys = jax.random.split(jax.random.fold_in(arg_keys[6], part), 7)
    volume = centred(own_keys[0], (S, NX, C, NY, NZ), 1.0, 6.0, ((0, 2), (1, 8)))
    cotangent = centred(own_keys[1], (S, NX, C, NY, NZ), 1.0, 6.0, ((0, 2), (1, 8)))
    spectral_weight = draw_spectral_weight(jax.random.fold_in(arg_keys[6], 71), part)
    pointwise_weight = centred(arg_keys[3], (C, C), C ** -0.5, 1.0)
    gain_table = jnp.clip(1.0 + 0.18 * jax.random.normal(arg_keys[4], (BIAS, C), jnp.float32), 0.099609375, 1.8984375).astype(jnp.bfloat16)
    bias_index = jax.random.randint(own_keys[5], (S,), 0, BIAS).astype(jnp.int32)
    return {"volume": volume, "cotangent": cotangent, "spectral_weight": spectral_weight, "pointwise_weight": pointwise_weight, "gain_table": gain_table, "bias_index": bias_index}


def trig_tables(length, modes_count, signed):
    positions = jnp.arange(length, dtype=jnp.int32)
    mode_base = jnp.arange(modes_count, dtype=jnp.int32)
    if signed:
        frequency = jnp.concatenate([mode_base, mode_base - modes_count])
    else:
        frequency = mode_base
    phase_index = jnp.mod(positions[:, None] * frequency[None, :], length)
    angles = phase_index.astype(jnp.float32) * (2.0 * math.pi / length)
    return (jnp.cos(angles).astype(jnp.bfloat16), jnp.sin(angles).astype(jnp.bfloat16))

def to_float(array_in):
    return array_in.astype(jnp.float32)

def reference(volume, cotangent, spectral_weight, pointwise_weight, gain_table, bias_index):
    cos_z, sin_z = trig_tables(NZ, M, False)
    cos_y, sin_y = trig_tables(NY, M, True)
    cos_x, sin_x = trig_tables(NX, M, True)
    cos_z, sin_z = (to_float(cos_z), to_float(sin_z))
    cos_y, sin_y = (to_float(cos_y), to_float(sin_y))
    cos_x, sin_x = (to_float(cos_x), to_float(sin_x))
    ortho_scale = 1.0 / math.sqrt(NX * NY * NZ)
    pair_total = 2 * M * M
    pair_index = jnp.arange(pair_total, dtype=jnp.int32)
    doubled_scale = jnp.where(pair_index % M == 0, 1.0, 2.0).astype(jnp.float32) * ortho_scale
    flat_scale = jnp.full((pair_total,), ortho_scale, dtype=jnp.float32)

    def lateral(values_in):
        source = to_float(values_in)
        real_z = jnp.einsum('xcyz,zd->xcyd', source, cos_z).astype(jnp.bfloat16)
        imag_z = (-jnp.einsum('xcyz,zd->xcyd', source, sin_z)).astype(jnp.bfloat16)
        real_z, imag_z = (to_float(real_z), to_float(imag_z))
        real_y = jnp.einsum('xcyd,yb->xcbd', real_z, cos_y) + jnp.einsum('xcyd,yb->xcbd', imag_z, sin_y)
        imag_y = jnp.einsum('xcyd,yb->xcbd', imag_z, cos_y) - jnp.einsum('xcyd,yb->xcbd', real_z, sin_y)
        return (real_y.astype(jnp.bfloat16).reshape(NX, C, pair_total), imag_y.astype(jnp.bfloat16).reshape(NX, C, pair_total))

    def axial(planes, pair_scale):
        plane_real, plane_imag = (to_float(planes[0]), to_float(planes[1]))
        real_h = jnp.einsum('sxcp,xa->sapc', plane_real, cos_x) + jnp.einsum('sxcp,xa->sapc', plane_imag, sin_x)
        imag_h = jnp.einsum('sxcp,xa->sapc', plane_imag, cos_x) - jnp.einsum('sxcp,xa->sapc', plane_real, sin_x)
        factor = pair_scale[None, None, :, None]
        return (to_float((real_h * factor).astype(jnp.bfloat16)), to_float((imag_h * factor).astype(jnp.bfloat16)))
    vol_real, vol_imag = axial(lax.map(lateral, volume), flat_scale)
    cot_real, cot_imag = axial(lax.map(lateral, cotangent), doubled_scale)
    grad_real = jnp.einsum('sapc,sapo->apco', vol_real, cot_real) + jnp.einsum('sapc,sapo->apco', vol_imag, cot_imag)
    grad_imag = jnp.einsum('sapc,sapo->apco', vol_real, cot_imag) - jnp.einsum('sapc,sapo->apco', vol_imag, cot_real)
    spectral_grad = jnp.stack([grad_real, grad_imag])
    weight_real = to_float(spectral_weight[0])
    weight_imag = to_float(spectral_weight[1])
    back_real = (jnp.einsum('apco,sapo->sapc', weight_real, cot_real) + jnp.einsum('apco,sapo->sapc', weight_imag, cot_imag)).astype(jnp.bfloat16)
    back_imag = (jnp.einsum('apco,sapo->sapc', weight_real, cot_imag) - jnp.einsum('apco,sapo->sapc', weight_imag, cot_real)).astype(jnp.bfloat16)
    back_real, back_imag = (to_float(back_real), to_float(back_imag))
    planes_real = (jnp.einsum('sapc,xa->sxcp', back_real, cos_x) - jnp.einsum('sapc,xa->sxcp', back_imag, sin_x)).astype(jnp.bfloat16)
    planes_imag = (jnp.einsum('sapc,xa->sxcp', back_real, sin_x) + jnp.einsum('sapc,xa->sxcp', back_imag, cos_x)).astype(jnp.bfloat16)
    gain_rows = to_float(gain_table[bias_index])

    def finish(members):
        plane_re, plane_im, grad_out, gain_row = members
        grid_real = to_float(plane_re).reshape(NX, C, 2 * M, M)
        grid_imag = to_float(plane_im).reshape(NX, C, 2 * M, M)
        row_real = (jnp.einsum('xcbd,yb->xcyd', grid_real, cos_y) - jnp.einsum('xcbd,yb->xcyd', grid_imag, sin_y)).astype(jnp.bfloat16)
        row_imag = (jnp.einsum('xcbd,yb->xcyd', grid_real, sin_y) + jnp.einsum('xcbd,yb->xcyd', grid_imag, cos_y)).astype(jnp.bfloat16)
        spectral_part = (jnp.einsum('xcyd,zd->xcyz', to_float(row_real), cos_z) - jnp.einsum('xcyd,zd->xcyz', to_float(row_imag), sin_z)) * ortho_scale
        scaled = (to_float(grad_out) * gain_row[None, :, None, None]).astype(jnp.bfloat16)
        pointwise_part = jnp.einsum('co,xoyz->xcyz', to_float(pointwise_weight), to_float(scaled))
        return (spectral_part + pointwise_part).astype(jnp.bfloat16)
    input_grad = lax.map(finish, (planes_real, planes_imag, cotangent, gain_rows))
    return (input_grad, spectral_grad)
```

```python
import functools
import math

import jax
import jax.numpy as jnp
import numpy as np
from jax import lax
from jax.experimental import pallas as pl
from jax.experimental.pallas import tpu as pltpu
from jax.sharding import PartitionSpec as P

M = 16
NX = 128
NY = 128
NZ = 128


def trig_tables(length, modes_count, signed):
    positions = jnp.arange(length, dtype=jnp.int32)
    mode_base = jnp.arange(modes_count, dtype=jnp.int32)
    if signed:
        frequency = jnp.concatenate([mode_base, mode_base - modes_count])
    else:
        frequency = mode_base
    phase_index = jnp.mod(positions[:, None] * frequency[None, :], length)
    angles = phase_index.astype(jnp.float32) * (2.0 * math.pi / length)
    return (jnp.cos(angles).astype(jnp.bfloat16), jnp.sin(angles).astype(jnp.bfloat16))


def general_device(volume, cotangent, spectral_weight, pointwise_weight, gain_table, bias_index):
    cos_z, sin_z = trig_tables(NZ, M, False)
    cos_y, sin_y = trig_tables(NY, M, True)
    cos_x, sin_x = trig_tables(NX, M, True)
    table_z = jnp.concatenate([cos_z, -sin_z], axis=1)
    table_y = jnp.concatenate([cos_y, sin_y], axis=1)
    paired_y = jnp.stack([cos_y, sin_y], axis=1)
    table_x = jnp.concatenate([cos_x, sin_x], axis=1)
    paired_x = jnp.stack([cos_x, sin_x], axis=1)
    ortho_scale = 1.0 / math.sqrt(NX * NY * NZ)
    pair_count = spectral_weight.shape[2]
    global_pairs = lax.axis_index("space") * pair_count + jnp.arange(pair_count, dtype=jnp.int32)
    flat_scale = jnp.full((pair_count,), ortho_scale, dtype=jnp.float32)
    doubled_scale = jnp.where(global_pairs % M == 0, 1.0, 2.0).astype(jnp.float32) * ortho_scale

    def lateral_spectrum(values_in):
        along_z = jnp.einsum(
            "sxcyz,zk->sxcky", values_in, table_z, preferred_element_type=jnp.float32
        ).astype(jnp.bfloat16)
        products = jnp.einsum(
            "sxcky,yj->sxckj", along_z, table_y, preferred_element_type=jnp.float32
        )
        real_part = products[:, :, :, :M, : 2 * M] + products[:, :, :, M:, 2 * M :]
        imag_part = products[:, :, :, M:, : 2 * M] - products[:, :, :, :M, 2 * M :]
        stacked = jnp.swapaxes(jnp.stack([real_part, imag_part], axis=2), 4, 5).astype(jnp.bfloat16)
        return stacked.reshape(stacked.shape[0], stacked.shape[1], 2, stacked.shape[3], 2 * M * M)

    def axial_spectrum(received, pair_scale):
        products = jnp.einsum(
            "sxrcp,xj->srjpc", received, table_x, preferred_element_type=jnp.float32
        )
        real_part = products[:, 0, : 2 * M] + products[:, 1, 2 * M :]
        imag_part = products[:, 1, : 2 * M] - products[:, 0, 2 * M :]
        stacked = jnp.stack([real_part, imag_part], axis=1)
        return (stacked * pair_scale[None, None, None, :, None]).astype(jnp.bfloat16)

    volume_hat = axial_spectrum(
        lax.all_to_all(lateral_spectrum(volume), "space", split_axis=4, concat_axis=1, tiled=True),
        flat_scale,
    )
    cotangent_hat = axial_spectrum(
        lax.all_to_all(
            lateral_spectrum(cotangent), "space", split_axis=4, concat_axis=1, tiled=True
        ),
        doubled_scale,
    )
    grad_real = jnp.einsum(
        "sapc,sapo->apco", volume_hat[:, 0], cotangent_hat[:, 0], preferred_element_type=jnp.float32
    ) + jnp.einsum(
        "sapc,sapo->apco", volume_hat[:, 1], cotangent_hat[:, 1], preferred_element_type=jnp.float32
    )
    grad_imag = jnp.einsum(
        "sapc,sapo->apco", volume_hat[:, 0], cotangent_hat[:, 1], preferred_element_type=jnp.float32
    ) - jnp.einsum(
        "sapc,sapo->apco", volume_hat[:, 1], cotangent_hat[:, 0], preferred_element_type=jnp.float32
    )
    spectral_grad = lax.psum_scatter(
        jnp.stack([grad_real, grad_imag]).astype(jnp.bfloat16),
        "dp",
        scatter_dimension=4,
        tiled=True,
    ).astype(jnp.float32)
    weight_real = spectral_weight[0]
    weight_imag = spectral_weight[1]
    cot_real = cotangent_hat[:, 0]
    cot_imag = cotangent_hat[:, 1]
    back_real = jnp.einsum(
        "apco,sapo->sapc", weight_real, cot_real, preferred_element_type=jnp.float32
    ) + jnp.einsum("apco,sapo->sapc", weight_imag, cot_imag, preferred_element_type=jnp.float32)
    back_imag = jnp.einsum(
        "apco,sapo->sapc", weight_real, cot_imag, preferred_element_type=jnp.float32
    ) - jnp.einsum("apco,sapo->sapc", weight_imag, cot_real, preferred_element_type=jnp.float32)
    back_modes = jnp.stack([back_real, back_imag], axis=1).astype(jnp.bfloat16)
    products = jnp.einsum(
        "srapc,xta->srtxcp", back_modes, paired_x, preferred_element_type=jnp.float32
    )
    plane_real = products[:, 0, 0] - products[:, 1, 1]
    plane_imag = products[:, 0, 1] + products[:, 1, 0]
    back_planes = jnp.stack([plane_real, plane_imag], axis=2).astype(jnp.bfloat16)
    received = lax.all_to_all(back_planes, "space", split_axis=1, concat_axis=4, tiled=True)
    mode_grid = received.reshape(
        received.shape[0], received.shape[1], 2, received.shape[3], 2 * M, M
    )
    row_products = jnp.einsum(
        "nxrcbd,ytb->nxrtcyd", mode_grid, paired_y, preferred_element_type=jnp.float32
    )
    row_real = row_products[:, :, 0, 0] - row_products[:, :, 1, 1]
    row_imag = row_products[:, :, 0, 1] + row_products[:, :, 1, 0]
    row_values = jnp.concatenate([row_real, row_imag], axis=4).astype(jnp.bfloat16)
    spectral_part = (
        jnp.einsum("nxcyk,kz->nxcyz", row_values, table_z.T, preferred_element_type=jnp.float32)
        * ortho_scale
    )
    bias_rows = (
        bias_index[:, None] == jnp.arange(gain_table.shape[0], dtype=jnp.int32)[None, :]
    ).astype(jnp.bfloat16)
    gain_rows = jnp.dot(bias_rows, gain_table, preferred_element_type=jnp.float32)
    scaled = (cotangent * gain_rows[:, None, :, None, None]).astype(jnp.bfloat16)
    pointwise_part = jnp.einsum(
        "co,sxoyz->sxcyz", pointwise_weight, scaled, preferred_element_type=jnp.float32
    )
    return ((spectral_part + pointwise_part).astype(jnp.bfloat16), spectral_grad)


BF = jnp.bfloat16
F32 = jnp.float32
ORTHO = 1.0 / math.sqrt(NX * NY * NZ)


def host_tables(length, modes_count, signed):
    frequency = np.arange(modes_count)
    if signed:
        frequency = np.concatenate([frequency, frequency - modes_count])
    phase = np.mod(np.arange(length)[:, None] * frequency[None, :], length)
    angles = phase.astype(np.float32) * np.float32(2.0 * math.pi / length)
    cos = np.cos(angles).astype(jnp.bfloat16).astype(np.float32)
    sin = np.sin(angles).astype(jnp.bfloat16).astype(np.float32)
    return cos, sin


def fixed_operands():
    cz, sz = host_tables(NZ, M, False)
    cy, sy = host_tables(NY, M, True)
    cx, sx = host_tables(NX, M, True)
    z_ops = np.zeros((8, NZ, 2, 8, M), np.float32)
    for c in range(8):
        z_ops[c, :, 0, c] = cz
        z_ops[c, :, 1, c] = -sz
    z_ops = z_ops.reshape(8 * NZ, 16 * M)
    y_fwd = np.concatenate(
        [np.concatenate([cy.T, sy.T], 1), np.concatenate([-sy.T, cy.T], 1)], 0
    )
    x_fwd = np.concatenate(
        [np.concatenate([cx.T, sx.T], 1), np.concatenate([-sx.T, cx.T], 1)], 0
    )
    x_fwd = x_fwd.reshape(2, M, 2, 2 * NX).transpose(2, 0, 1, 3).reshape(4 * M, 2 * NX)
    x_back = np.concatenate(
        [np.concatenate([cx, -sx], 1), np.concatenate([sx, cx], 1)], 0
    )
    x_back = x_back.reshape(2 * NX, 2, M, 2).transpose(0, 3, 1, 2).reshape(2 * NX, 4 * M)
    y_back = np.stack(
        [np.concatenate([cy, sy], 0), np.concatenate([-sy, cy], 0)], 2
    ).reshape(2 * NY, 4 * M)
    shuffle = np.zeros((4, 8, M, 8, 2, 4, M), np.float32)
    for b in range(4):
        for c in range(8):
            for d in range(M):
                shuffle[b, c, d, c, :, b, d] = 1.0
    shuffle = shuffle.reshape(32 * M, 64 * M)
    ops = dict(
        z_fwd=z_ops, z_back=z_ops.T, y_fwd=y_fwd, x_fwd=x_fwd, x_back=x_back,
        y_back=y_back, spread=shuffle, gather=shuffle.T,
    )
    return {k: jnp.asarray(np.ascontiguousarray(v).astype(jnp.bfloat16)) for k, v in ops.items()}


def dot(a, b):
    return jnp.dot(a, b, preferred_element_type=F32)


def params(mib):
    return pltpu.CompilerParams(vmem_limit_bytes=mib << 20)


def whole(shape):
    return pl.BlockSpec(shape, lambda *i: (0,) * len(shape))


def lateral_kernel(v_ref, z_ref, y_ref, o_ref, s_ref):
    i = pl.program_id(0)
    nx = pl.num_programs(0)
    rows = [
        jnp.concatenate([v_ref[0, co * 8 + c] for c in range(8)], axis=1) for co in range(4)
    ]
    along = dot(jnp.concatenate(rows, axis=0), z_ref[...]).astype(BF)
    for h in range(2):
        lo = along[h * 256 : h * 256 + 128]
        hi = along[h * 256 + 128 : h * 256 + 256]
        rhs = jnp.concatenate(
            [
                jnp.concatenate([lo[:, :128], hi[:, :128]], axis=1),
                jnp.concatenate([lo[:, 128:], hi[:, 128:]], axis=1),
            ],
            axis=0,
        )
        plane = dot(y_ref[...], rhs)
        for j in range(2):
            s_ref[h * 2 + j, pl.ds(pl.multiple_of(i * 64, 64), 64), :] = plane[
                :, j * 128 : j * 128 + 128
            ]

    @pl.when(i == nx - 1)
    def _():
        for r in range(64):
            part, b = divmod(r, 32)
            lane = ((b % 4) * 2 + part) * 512
            for q in range(4):
                o_ref[b // 4, :, lane + q * 128 : lane + q * 128 + 128] = s_ref[
                    q, pl.ds(r, 16, stride=64), :
                ].astype(BF)


def lateral(values, ops):
    nx = values.shape[0]
    return pl.pallas_call(
        lateral_kernel,
        grid=(nx,),
        in_specs=[
            pl.BlockSpec((1, 32, NY, NZ), lambda i: (i, 0, 0, 0)),
            whole((1024, 256)),
            whole((64, 256)),
        ],
        out_specs=whole((8, nx, 4096)),
        out_shape=jax.ShapeDtypeStruct((8, nx, 4096), BF),
        scratch_shapes=[pltpu.VMEM((4, nx * 64, 128), F32)],
        compiler_params=params(32),
        cost_estimate=pl.CostEstimate(
            flops=2 * nx * 4096 * 128 * 256, bytes_accessed=nx * (1 << 20), transcendentals=0
        ),
        name="lateral",
    )(values, ops["z_fwd"], ops["y_fwd"])


def axial_modes(r_ref, x_ref, spread_ref, doubled, store):
    lane = lax.broadcasted_iota(jnp.int32, (1, 512), 1)
    scale = jnp.where(lane % M == 0, ORTHO, (2.0 if doubled else 1.0) * ORTHO).astype(F32)
    cuts = []
    for b in range(4):
        rhs = jnp.concatenate(
            [r_ref[:, pl.ds(b * 1024, 512)], r_ref[:, pl.ds(b * 1024 + 512, 512)]], axis=0
        )
        cuts.append((dot(x_ref[...], rhs) * scale).astype(BF))
    even, odd = [
        jnp.concatenate(
            [
                jnp.concatenate(
                    [cut[a2 * 32 : a2 * 32 + 32, co * 128 : co * 128 + 128] for cut in cuts],
                    axis=1,
                )
                for co in range(4)
            ],
            axis=0,
        )
        for a2 in range(2)
    ]
    both = jnp.concatenate([even, odd], axis=0)
    low = lax.broadcasted_iota(jnp.int32, (128, 128), 1) < 64
    for c in range(8):
        moved = dot(both, spread_ref[:, pl.ds(c * 128, 128)])
        store(c, jnp.where(low, moved[:128], moved[128:]))


def volume_modes_kernel(r_ref, x_ref, spread_ref, o_ref):
    def store(c, value):
        for co in range(4):
            o_ref[co * 8 + c] = value[co * 32 : co * 32 + 32].astype(BF)

    axial_modes(r_ref, x_ref, spread_ref, False, store)


def volume_modes(received, ops):
    return pl.pallas_call(
        volume_modes_kernel,
        out_shape=jax.ShapeDtypeStruct((32, 32, 128), BF),
        compiler_params=params(32),
        cost_estimate=pl.CostEstimate(flops=1 << 29, bytes_accessed=3 << 20, transcendentals=0),
        name="volume_modes",
    )(received.reshape(NX, 4096), ops["x_fwd"], ops["spread"])


def cotangent_modes_kernel(
    r_ref, w_ref, x_ref, spread_ref, gather_ref, xb_ref, g_ref, o_ref, g_s, b_s, t_s
):
    i = pl.program_id(0)

    @pl.when(i == 0)
    def _():
        def store(c, value):
            for co in range(4):
                cut = value[co * 32 : co * 32 + 32]
                g_ref[co * 8 + c] = cut.astype(BF)
                g_s[pl.ds((co * 8 + c) * 32, 32), :] = cut

        axial_modes(r_ref, x_ref, spread_ref, True, store)

    g_re = g_s[pl.ds(i, 32, stride=32), :]
    g_im = g_s[pl.ds(i + 16, 32, stride=32), :]

    def one(c, carry):
        w_re = jnp.concatenate([w_ref[0, 0, c], w_ref[0, 1, c]], axis=1).astype(F32)
        w_im = jnp.concatenate([w_ref[1, 0, c], w_ref[1, 1, c]], axis=1).astype(F32)
        re = w_re * g_re + w_im * g_im
        im = w_re * g_im - w_im * g_re
        row = pl.multiple_of(c * 8, 8)
        t_s[0, pl.ds(row, 8), :] = (re[:8] + re[8:16]) + (re[16:24] + re[24:])
        t_s[1, pl.ds(row, 8), :] = (im[:8] + im[8:16]) + (im[16:24] + im[24:])
        return carry

    lax.fori_loop(0, 32, one, 0, unroll=8)
    for part in range(2):
        total = t_s[part, pl.ds(0, 32, stride=8), :]
        for k in range(1, 8):
            total = total + t_s[part, pl.ds(k, 32, stride=8), :]
        b_s[pl.ds(pl.multiple_of((part * 16 + i) * 32, 32), 32), :] = total * ORTHO

    @pl.when(i == pl.num_programs(0) - 1)
    def _():
        low = lax.broadcasted_iota(jnp.int32, (32, 128), 1) < 64
        stacks = [[], []]
        for co in range(4):
            cuts = [b_s[pl.ds(co * 8 + c, 32, stride=32), :] for c in range(8)]
            for a2 in range(2):
                keep = low if a2 == 0 else jnp.logical_not(low)
                stacks[a2].append(
                    jnp.concatenate([jnp.where(keep, cut, 0.0).astype(BF) for cut in cuts], axis=1)
                )
        moved = dot(jnp.concatenate(stacks[0] + stacks[1], axis=0), gather_ref[...]).astype(BF)
        for co in range(4):
            rhs = jnp.concatenate(
                [moved[co * 32 : co * 32 + 32], moved[128 + co * 32 : 128 + co * 32 + 32]], axis=0
            )
            planes = dot(xb_ref[...], rhs).astype(BF)
            for part in range(2):
                for b in range(4):
                    lane = (b * 2 + part) * 512 + co * 128
                    o_ref[:, lane : lane + 128] = planes[
                        part * 128 : part * 128 + 128, b * 128 : b * 128 + 128
                    ]


def cotangent_modes(received, weight, ops):
    return pl.pallas_call(
        cotangent_modes_kernel,
        grid=(M,),
        in_specs=[
            whole((NX, 4096)),
            pl.BlockSpec((2, 2, 32, 32, 64), lambda i: (0, i, 0, 0, 0)),
            whole((64, 256)),
            whole((512, 1024)),
            whole((1024, 512)),
            whole((256, 64)),
        ],
        out_specs=[whole((32, 32, 128)), whole((NX, 4096))],
        out_shape=[
            jax.ShapeDtypeStruct((32, 32, 128), BF),
            jax.ShapeDtypeStruct((NX, 4096), BF),
        ],
        scratch_shapes=[
            pltpu.VMEM((1024, 128), F32),
            pltpu.VMEM((1024, 128), F32),
            pltpu.VMEM((2, 256, 128), F32),
        ],
        compiler_params=params(40),
        cost_estimate=pl.CostEstimate(flops=1 << 31, bytes_accessed=20 << 20, transcendentals=0),
        name="cotangent_modes",
    )(
        received.reshape(NX, 4096),
        weight,
        ops["x_fwd"],
        ops["spread"],
        ops["gather"],
        ops["x_back"],
    )


def weight_grad_kernel(half_ref, u0_ref, u1_ref, g0_ref, g1_ref, o_ref, u_s, g_s):
    i = pl.program_id(0)

    @pl.when(i == 0)
    def _():
        for s, (u, g) in enumerate(((u0_ref, g0_ref), (u1_ref, g1_ref))):
            u_s[s] = u[...].reshape(1024, 128).astype(F32)
            g_s[s] = g[...].reshape(1024, 128).astype(F32)

    base = half_ref[0] * 512
    u = [[u_s[s, pl.ds(i + 16 * r, 32, stride=32), :] for r in range(2)] for s in range(2)]
    g = [[g_s[s, pl.ds(base + i + 16 * r, 16, stride=32), :] for r in range(2)] for s in range(2)]
    for c in range(32):
        row = [[jnp.broadcast_to(u[s][r][c : c + 1], (16, 128)) for r in range(2)] for s in range(2)]
        re = (row[0][0] * g[0][0] + row[0][1] * g[0][1]) + (
            row[1][0] * g[1][0] + row[1][1] * g[1][1]
        )
        im = (row[0][0] * g[0][1] - row[0][1] * g[0][0]) + (
            row[1][0] * g[1][1] - row[1][1] * g[1][0]
        )
        o_ref[0, 0, c] = re[:, :64]
        o_ref[0, 1, c] = re[:, 64:]
        o_ref[1, 0, c] = im[:, :64]
        o_ref[1, 1, c] = im[:, 64:]


def weight_grad(half, u0, u1, g0, g1):
    shape = (32, 32, 128)
    return pl.pallas_call(
        weight_grad_kernel,
        grid_spec=pltpu.PrefetchScalarGridSpec(
            num_scalar_prefetch=1,
            grid=(M,),
            in_specs=[whole(shape)] * 4,
            out_specs=pl.BlockSpec((2, 2, 32, 16, 64), lambda i, h: (0, i, 0, 0, 0)),
            scratch_shapes=[pltpu.VMEM((2, 1024, 128), F32), pltpu.VMEM((2, 1024, 128), F32)],
        ),
        out_shape=jax.ShapeDtypeStruct((2, 32, 32, 16, 64), F32),
        compiler_params=params(32),
        cost_estimate=pl.CostEstimate(flops=1 << 25, bytes_accessed=18 << 20, transcendentals=0),
        name="weight_grad",
    )(half, u0, u1, g0, g1)


def finish_kernel(r_ref, v_ref, k_ref, y_ref, z_ref, o_ref, s_ref, a_ref):
    i = pl.program_id(0)

    @pl.when(i == 0)
    def _():
        for src in range(8):
            for k in range(8):
                for q in range(4):
                    s_ref[q, pl.ds(src * 8 + k, 16, stride=64), :] = r_ref[
                        src, :, pl.ds(k * 512 + q * 128, 128)
                    ].astype(F32)

    planes = jnp.concatenate(
        [s_ref[q, pl.ds(pl.multiple_of(i * 64, 64), 64), :].astype(BF) for q in range(4)], axis=1
    )
    rows = dot(y_ref[...], planes).astype(BF)
    lhs = jnp.concatenate(
        [
            jnp.concatenate(
                [rows[:128, co * 128 : co * 128 + 128], rows[128:, co * 128 : co * 128 + 128]],
                axis=1,
            )
            for co in range(4)
        ],
        axis=0,
    )
    for n in range(4):
        part = dot(lhs, z_ref[:, pl.ds(n * 256, 256)])
        for co in range(4):
            for j in range(2):
                a_ref[co * 8 + n * 2 + j] = part[
                    co * 128 : co * 128 + 128, j * 128 : j * 128 + 128
                ]
    for y in range(8):
        cut = v_ref[0, :, pl.ds(y * 16, 16), :].astype(F32)
        rhs = jnp.concatenate(
            [
                cut[:, :8].reshape(256, 128).astype(BF),
                cut[:, 8:].reshape(256, 128).astype(BF),
            ],
            axis=1,
        )
        point = dot(k_ref[...], rhs)
        point = jnp.concatenate(
            [point[:, :128].reshape(32, 8, 128), point[:, 128:].reshape(32, 8, 128)], axis=1
        )
        o_ref[0, :, pl.ds(y * 16, 16), :] = (point + a_ref[:, pl.ds(y * 16, 16), :]).astype(BF)


def finish(received, cotangent, point_kron, ops):
    nx = cotangent.shape[0]
    return pl.pallas_call(
        finish_kernel,
        grid=(nx,),
        in_specs=[
            whole((8, nx, 4096)),
            pl.BlockSpec((1, 32, NY, NZ), lambda i: (i, 0, 0, 0)),
            whole((256, 256)),
            whole((256, 64)),
            whole((256, 1024)),
        ],
        out_specs=pl.BlockSpec((1, 32, NY, NZ), lambda i: (i, 0, 0, 0)),
        out_shape=jax.ShapeDtypeStruct(cotangent.shape, BF),
        scratch_shapes=[pltpu.VMEM((4, nx * 64, 128), F32), pltpu.VMEM((32, NY, NZ), F32)],
        compiler_params=params(40),
        cost_estimate=pl.CostEstimate(
            flops=nx * (1 << 29), bytes_accessed=nx * (2 << 20), transcendentals=0
        ),
        name="finish",
    )(received, cotangent, point_kron, ops["y_back"], ops["z_back"])


def exchange(blocks):
    return lax.all_to_all(blocks, "space", split_axis=0, concat_axis=0, tiled=True)


def tuned_device(volume, cotangent, spectral_weight, pointwise_weight, gain_table, bias_index):
    ops = fixed_operands()
    nx = volume.shape[1]
    vol = volume.reshape(nx, 32, NY, NZ)
    cot = cotangent.reshape(nx, 32, NY, NZ)
    cot_received = exchange(lateral(cot, ops))
    vol_received = exchange(lateral(vol, ops))
    weight = jnp.transpose(spectral_weight, (0, 1, 3, 4, 2))
    g_modes, planes = cotangent_modes(cot_received, weight, ops)
    back = exchange(planes.reshape(8, nx, 4096))
    u_modes = volume_modes(vol_received, ops)
    swap = [(0, 1), (1, 0)]
    g_other = lax.ppermute(g_modes, "dp", swap)
    u_other = lax.ppermute(u_modes, "dp", swap)
    half = lax.axis_index("dp").astype(jnp.int32).reshape(1)
    grad = weight_grad(half, u_modes, u_other, g_modes, g_other)
    gain = gain_table[bias_index[0]].astype(F32)
    folded = (pointwise_weight.astype(F32) * gain[None, :]).astype(BF)
    eye = jnp.eye(8, dtype=BF)
    point_kron = (folded[:, None, :, None] * eye[None, :, None, :]).reshape(256, 256)
    out = finish(back, cot, point_kron, ops)
    return out.reshape(volume.shape), jnp.transpose(grad, (0, 1, 4, 2, 3))


def per_device(volume, cotangent, spectral_weight, pointwise_weight, gain_table, bias_index):
    fits = (
        volume.shape == (1, 16, 32, NY, NZ)
        and spectral_weight.shape == (2, 2 * M, 64, 32, 32)
        and lax.axis_size("space") == 8
        and lax.axis_size("dp") == 2
    )
    device = tuned_device if fits else general_device
    return device(
        volume, cotangent, spectral_weight, pointwise_weight, gain_table, bias_index
    )


def solution(mesh):
    return jax.shard_map(
        per_device,
        mesh=mesh,
        in_specs=(
            P(("parts", "dp"), "space", None, None, None),
            P(("parts", "dp"), "space", None, None, None),
            P(None, None, "space", None, None),
            P(),
            P(),
            P(("parts", "dp")),
        ),
        out_specs=(
            P(("parts", "dp"), "space", None, None, None),
            P("parts", None, "space", None, "dp"),
        ),
        check_vma=False,
    )
```

```python
import functools
import math

import jax
import jax.numpy as jnp
import numpy as np
from jax import lax
from jax.experimental import pallas as pl
from jax.experimental.pallas import tpu as pltpu
from jax.sharding import PartitionSpec as P

M = 16
NX = 128
NY = 128
NZ = 128


def trig_tables(length, modes_count, signed):
    positions = jnp.arange(length, dtype=jnp.int32)
    mode_base = jnp.arange(modes_count, dtype=jnp.int32)
    if signed:
        frequency = jnp.concatenate([mode_base, mode_base - modes_count])
    else:
        frequency = mode_base
    phase_index = jnp.mod(positions[:, None] * frequency[None, :], length)
    angles = phase_index.astype(jnp.float32) * (2.0 * math.pi / length)
    return (jnp.cos(angles).astype(jnp.bfloat16), jnp.sin(angles).astype(jnp.bfloat16))


def general_device(volume, cotangent, spectral_weight, pointwise_weight, gain_table, bias_index):
    cos_z, sin_z = trig_tables(NZ, M, False)
    cos_y, sin_y = trig_tables(NY, M, True)
    cos_x, sin_x = trig_tables(NX, M, True)
    table_z = jnp.concatenate([cos_z, -sin_z], axis=1)
    table_y = jnp.concatenate([cos_y, sin_y], axis=1)
    paired_y = jnp.stack([cos_y, sin_y], axis=1)
    table_x = jnp.concatenate([cos_x, sin_x], axis=1)
    paired_x = jnp.stack([cos_x, sin_x], axis=1)
    ortho_scale = 1.0 / math.sqrt(NX * NY * NZ)
    pair_count = spectral_weight.shape[2]
    global_pairs = lax.axis_index("space") * pair_count + jnp.arange(pair_count, dtype=jnp.int32)
    flat_scale = jnp.full((pair_count,), ortho_scale, dtype=jnp.float32)
    doubled_scale = jnp.where(global_pairs % M == 0, 1.0, 2.0).astype(jnp.float32) * ortho_scale

    def lateral_spectrum(values_in):
        along_z = jnp.einsum(
            "sxcyz,zk->sxcky", values_in, table_z, preferred_element_type=jnp.float32
        ).astype(jnp.bfloat16)
        products = jnp.einsum(
            "sxcky,yj->sxckj", along_z, table_y, preferred_element_type=jnp.float32
        )
        real_part = products[:, :, :, :M, : 2 * M] + products[:, :, :, M:, 2 * M :]
        imag_part = products[:, :, :, M:, : 2 * M] - products[:, :, :, :M, 2 * M :]
        stacked = jnp.swapaxes(jnp.stack([real_part, imag_part], axis=2), 4, 5).astype(jnp.bfloat16)
        return stacked.reshape(stacked.shape[0], stacked.shape[1], 2, stacked.shape[3], 2 * M * M)

    def axial_spectrum(received, pair_scale):
        products = jnp.einsum(
            "sxrcp,xj->srjpc", received, table_x, preferred_element_type=jnp.float32
        )
        real_part = products[:, 0, : 2 * M] + products[:, 1, 2 * M :]
        imag_part = products[:, 1, : 2 * M] - products[:, 0, 2 * M :]
        stacked = jnp.stack([real_part, imag_part], axis=1)
        return (stacked * pair_scale[None, None, None, :, None]).astype(jnp.bfloat16)

    volume_hat = axial_spectrum(
        lax.all_to_all(lateral_spectrum(volume), "space", split_axis=4, concat_axis=1, tiled=True),
        flat_scale,
    )
    cotangent_hat = axial_spectrum(
        lax.all_to_all(
            lateral_spectrum(cotangent), "space", split_axis=4, concat_axis=1, tiled=True
        ),
        doubled_scale,
    )
    grad_real = jnp.einsum(
        "sapc,sapo->apco", volume_hat[:, 0], cotangent_hat[:, 0], preferred_element_type=jnp.float32
    ) + jnp.einsum(
        "sapc,sapo->apco", volume_hat[:, 1], cotangent_hat[:, 1], preferred_element_type=jnp.float32
    )
    grad_imag = jnp.einsum(
        "sapc,sapo->apco", volume_hat[:, 0], cotangent_hat[:, 1], preferred_element_type=jnp.float32
    ) - jnp.einsum(
        "sapc,sapo->apco", volume_hat[:, 1], cotangent_hat[:, 0], preferred_element_type=jnp.float32
    )
    spectral_grad = lax.psum_scatter(
        jnp.stack([grad_real, grad_imag]).astype(jnp.bfloat16),
        "dp",
        scatter_dimension=4,
        tiled=True,
    ).astype(jnp.float32)
    weight_real = spectral_weight[0]
    weight_imag = spectral_weight[1]
    cot_real = cotangent_hat[:, 0]
    cot_imag = cotangent_hat[:, 1]
    back_real = jnp.einsum(
        "apco,sapo->sapc", weight_real, cot_real, preferred_element_type=jnp.float32
    ) + jnp.einsum("apco,sapo->sapc", weight_imag, cot_imag, preferred_element_type=jnp.float32)
    back_imag = jnp.einsum(
        "apco,sapo->sapc", weight_real, cot_imag, preferred_element_type=jnp.float32
    ) - jnp.einsum("apco,sapo->sapc", weight_imag, cot_real, preferred_element_type=jnp.float32)
    back_modes = jnp.stack([back_real, back_imag], axis=1).astype(jnp.bfloat16)
    products = jnp.einsum(
        "srapc,xta->srtxcp", back_modes, paired_x, preferred_element_type=jnp.float32
    )
    plane_real = products[:, 0, 0] - products[:, 1, 1]
    plane_imag = products[:, 0, 1] + products[:, 1, 0]
    back_planes = jnp.stack([plane_real, plane_imag], axis=2).astype(jnp.bfloat16)
    received = lax.all_to_all(back_planes, "space", split_axis=1, concat_axis=4, tiled=True)
    mode_grid = received.reshape(
        received.shape[0], received.shape[1], 2, received.shape[3], 2 * M, M
    )
    row_products = jnp.einsum(
        "nxrcbd,ytb->nxrtcyd", mode_grid, paired_y, preferred_element_type=jnp.float32
    )
    row_real = row_products[:, :, 0, 0] - row_products[:, :, 1, 1]
    row_imag = row_products[:, :, 0, 1] + row_products[:, :, 1, 0]
    row_values = jnp.concatenate([row_real, row_imag], axis=4).astype(jnp.bfloat16)
    spectral_part = (
        jnp.einsum("nxcyk,kz->nxcyz", row_values, table_z.T, preferred_element_type=jnp.float32)
        * ortho_scale
    )
    bias_rows = (
        bias_index[:, None] == jnp.arange(gain_table.shape[0], dtype=jnp.int32)[None, :]
    ).astype(jnp.bfloat16)
    gain_rows = jnp.dot(bias_rows, gain_table, preferred_element_type=jnp.float32)
    scaled = (cotangent * gain_rows[:, None, :, None, None]).astype(jnp.bfloat16)
    pointwise_part = jnp.einsum(
        "co,sxoyz->sxcyz", pointwise_weight, scaled, preferred_element_type=jnp.float32
    )
    return ((spectral_part + pointwise_part).astype(jnp.bfloat16), spectral_grad)


BF = jnp.bfloat16
F32 = jnp.float32
ORTHO = 1.0 / math.sqrt(NX * NY * NZ)


def host_tables(length, modes_count, signed):
    frequency = np.arange(modes_count)
    if signed:
        frequency = np.concatenate([frequency, frequency - modes_count])
    phase = np.mod(np.arange(length)[:, None] * frequency[None, :], length)
    angles = phase.astype(np.float32) * np.float32(2.0 * math.pi / length)
    cos = np.cos(angles).astype(jnp.bfloat16).astype(np.float32)
    sin = np.sin(angles).astype(jnp.bfloat16).astype(np.float32)
    return cos, sin


def fixed_operands():
    cz, sz = host_tables(NZ, M, False)
    cy, sy = host_tables(NY, M, True)
    cx, sx = host_tables(NX, M, True)
    z_ops = np.zeros((8, NZ, 2, 8, M), np.float32)
    for c in range(8):
        z_ops[c, :, 0, c] = cz
        z_ops[c, :, 1, c] = -sz
    z_ops = z_ops.reshape(8 * NZ, 16 * M)
    y_all = np.stack([np.concatenate([cy.T, sy.T], 1), np.concatenate([-sy.T, cy.T], 1)], 1)
    y_all = y_all.reshape(8, 4, 2, 2 * NY)
    x_all = np.stack([np.stack([cx.T, sx.T], 1), np.stack([-sx.T, cx.T], 1)], 0)
    x_all = x_all.reshape(2, M, 2, 2, 8, 16).transpose(2, 0, 1, 3, 4, 5)
    order = [[[s ^ (4 * j + k) for j in range(2)] for k in range(4)] for s in range(8)]
    y_ops = np.stack([y_all[order[s]] for s in range(8)]).reshape(8, 64, 2 * NY)
    x_ops = np.stack([x_all[..., [s ^ k for k in range(4)], :] for s in range(8)])
    x_ops = x_ops.reshape(8, 64, NX)
    shuffle = np.zeros((4, 8, M, 8, 2, 4, M), np.float32)
    for b in range(4):
        for c in range(8):
            for d in range(M):
                shuffle[b, c, d, c, :, b, d] = 1.0
    shuffle = shuffle.reshape(32 * M, 64 * M)
    ops = dict(z_fwd=z_ops, z_back=z_ops.T, y=y_ops, x=x_ops, spread=shuffle)
    return {k: jnp.asarray(np.ascontiguousarray(v).astype(jnp.bfloat16)) for k, v in ops.items()}


def dot(a, b):
    return jnp.dot(a, b, preferred_element_type=F32)


def params(mib):
    return pltpu.CompilerParams(vmem_limit_bytes=mib << 20)


def cost(us, mib=1):
    return pl.CostEstimate(
        flops=int(us * 6e6), bytes_accessed=mib << 10, transcendentals=0
    )


VMEM = pl.BlockSpec(memory_space=pltpu.VMEM)
SMEM = pl.BlockSpec(memory_space=pltpu.SMEM)
HBM = pl.BlockSpec(memory_space=pltpu.HBM)
UNREAD = pl.BlockSpec(memory_space=pl.ANY)


def in_vmem(x):
    return pltpu.with_memory_space_constraint(x, pltpu.VMEM)


def in_hbm(x):
    return pltpu.with_memory_space_constraint(x, pltpu.HBM)


GROUP = 4
SLOTS = 12


def lateral_kernel(me_ref, v_ref, z_hbm, y_hbm, _, *rest):
    outs, (s_ref, z_ref, y_ref, b_ref, sem, z_sem) = rest[:4], rest[4:]
    nx = v_ref.shape[0]

    def copy(x):
        slot = lax.rem(x, SLOTS)
        return pltpu.make_async_copy(v_ref.at[x], b_ref.at[slot], sem.at[slot])

    tables = [
        pltpu.make_async_copy(z_hbm, z_ref, z_sem.at[0]),
        pltpu.make_async_copy(y_hbm.at[me_ref[0]], y_ref, z_sem.at[1]),
    ]
    for x in range(GROUP):
        copy(x).start()
    for table in tables:
        table.start()
    for x in range(GROUP, SLOTS - GROUP):
        copy(x).start()
    for table in tables:
        table.wait()

    def one(i, carry):
        for k in range(GROUP):
            x = i * GROUP + k
            ahead = x + SLOTS - GROUP

            @pl.when(ahead < nx)
            def _():
                copy(ahead).start()

            copy(x).wait()
        rows = [
            jnp.concatenate(
                [b_ref[lax.rem(i * GROUP + k, SLOTS), co * 8 + c] for c in range(8)], axis=1
            )
            for k in range(GROUP)
            for co in range(4)
        ]
        along = dot(jnp.concatenate(rows, axis=0), z_ref[...]).astype(BF)
        for k in range(GROUP):
            for h in range(2):
                at = (k * 2 + h) * 256
                lo = along[at : at + 128]
                hi = along[at + 128 : at + 256]
                rhs = jnp.concatenate(
                    [
                        jnp.concatenate([lo[:, :128], hi[:, :128]], axis=1),
                        jnp.concatenate([lo[:, 128:], hi[:, 128:]], axis=1),
                    ],
                    axis=0,
                )
                out = dot(y_ref[...], rhs)
                for j in range(2):
                    s_ref[h * 2 + j, pl.ds(i * GROUP + k, 64, stride=16), :] = out[
                        :, j * 128 : j * 128 + 128
                    ]
        return carry

    lax.fori_loop(0, nx // GROUP, one, 0)
    for r in range(64):
        q, j, k = r // 16, (r // 8) % 2, r % 8
        for n in range(4):
            cut = s_ref[n, r * 16 : r * 16 + 16, :].astype(BF)
            outs[q][j, :, k * 512 + n * 128 : k * 512 + n * 128 + 128] = cut


def lateral(me, values, ops, first, name):
    nx = values.shape[0]
    return pl.pallas_call(
        lateral_kernel,
        in_specs=[SMEM, HBM, HBM, HBM, UNREAD],
        out_specs=[VMEM] * 4,
        out_shape=[jax.ShapeDtypeStruct((2, nx, 4096), BF)] * 4,
        scratch_shapes=[
            pltpu.VMEM((4, nx * 64, 128), F32),
            pltpu.VMEM((1024, 256), BF),
            pltpu.VMEM((64, 256), BF),
            pltpu.VMEM((SLOTS, 32, NY, NZ), BF),
            pltpu.SemaphoreType.DMA((SLOTS,)),
            pltpu.SemaphoreType.DMA((2,)),
        ],
        compiler_params=params(20),
        cost_estimate=cost(10),
        name=name,
    )(me, in_hbm(values), in_hbm(ops["z_fwd"]), in_hbm(ops["y"]), first)


def square_sum(table, refs, j, b):
    rhs = jnp.concatenate(
        [ref[j, :, pl.ds(b * 1024 + part * 512, 512)] for part in range(2) for ref in refs],
        axis=0,
    )
    return dot(table, rhs)


def partner_kernel(me_ref, r0, r1, r2, r3, x_hbm, _, o_ref, __, x_ref, sem):
    copy = pltpu.make_async_copy(x_hbm.at[me_ref[0]], x_ref, sem)
    copy.start()
    copy.wait()
    for b in range(4):
        o_ref[:, pl.ds(b * 512, 512)] = square_sum(x_ref[...], (r0, r1, r2, r3), 1, b).astype(BF)


def partner_modes(me, received, ops, passed, name):
    return pl.pallas_call(
        partner_kernel,
        in_specs=[SMEM] + [VMEM] * 4 + [HBM, UNREAD],
        out_specs=[VMEM, UNREAD],
        out_shape=[
            jax.ShapeDtypeStruct((64, 2048), BF),
            jax.ShapeDtypeStruct(passed.shape, passed.dtype),
        ],
        input_output_aliases={6: 1},
        scratch_shapes=[pltpu.VMEM((64, NX), BF), pltpu.SemaphoreType.DMA(())],
        compiler_params=params(16),
        cost_estimate=cost(1),
        name=name,
    )(me, *received, in_hbm(ops["x"]), passed)


def axial_modes(table, refs, other_ref, spread_ref, ready, doubled, store):
    lane = lax.broadcasted_iota(jnp.int32, (1, 512), 1)
    scale = jnp.where(lane % M == 0, ORTHO, (2.0 if doubled else 1.0) * ORTHO).astype(F32)
    cuts = [
        (
            (square_sum(table, refs, 0, b) + other_ref[:, pl.ds(b * 512, 512)].astype(F32)) * scale
        ).astype(BF)
        for b in range(4)
    ]
    both = jnp.concatenate(
        [
            jnp.concatenate(
                [cut[a2 * 32 : a2 * 32 + 32, co * 128 : co * 128 + 128] for cut in cuts], axis=1
            )
            for a2 in range(2)
            for co in range(4)
        ],
        axis=0,
    )
    low = lax.broadcasted_iota(jnp.int32, (128, 128), 1) < 64
    ready()
    for c in range(0, 8, 2):
        moved = dot(both, spread_ref[:, pl.ds(c * 128, 256)])
        for k in range(2):
            cut = moved[:, k * 128 : k * 128 + 128]
            store(c + k, jnp.where(low, cut[:128], cut[128:]))


def volume_modes_kernel(
    me_ref, r0, r1, r2, r3, other_ref, x_hbm, spread_hbm, *rest
):
    o_ref, x_ref, spread_ref, sem = rest[-4:]
    copies = [
        pltpu.make_async_copy(x_hbm.at[me_ref[0]], x_ref, sem.at[0]),
        pltpu.make_async_copy(spread_hbm, spread_ref, sem.at[1]),
    ]
    for copy in copies:
        copy.start()

    def store(c, value):
        for co in range(4):
            o_ref[co * 8 + c] = value[co * 32 : co * 32 + 32].astype(BF)

    copies[0].wait()
    axial_modes(
        x_ref[...], (r0, r1, r2, r3), other_ref, spread_ref, copies[1].wait, False, store
    )


MODE_SCRATCH = [
    pltpu.VMEM((64, NX), BF),
    pltpu.VMEM((512, 1024), BF),
    pltpu.SemaphoreType.DMA((2,)),
]


def volume_modes(me, received, other, ops, ahead):
    return pl.pallas_call(
        volume_modes_kernel,
        in_specs=[SMEM] + [VMEM] * 5 + [HBM] * 2 + [UNREAD] * len(ahead),
        out_specs=VMEM,
        out_shape=jax.ShapeDtypeStruct((32, 32, 128), BF),
        scratch_shapes=MODE_SCRATCH,
        compiler_params=params(16),
        cost_estimate=cost(1.5),
        name="volume_modes",
    )(me, *received, other, in_hbm(ops["x"]), in_hbm(ops["spread"]), *ahead)


def kron_operand(at, p_ref, gain_ref):
    lane = lax.broadcasted_iota(jnp.int32, (32, 128), 1)
    here = lane == lax.rem(at, 128)
    gain = jnp.sum(jnp.where(here, gain_ref[...].astype(F32), 0.0), axis=1, keepdims=True)
    wide = (
        lax.broadcasted_iota(jnp.int32, (32, 256), 0)
        == lax.broadcasted_iota(jnp.int32, (32, 256), 1) // 8
    )
    tall = (
        lax.broadcasted_iota(jnp.int32, (256, 32), 0) // 8
        == lax.broadcasted_iota(jnp.int32, (256, 32), 1)
    )
    gains = jnp.sum(jnp.where(wide, gain, 0.0), axis=0, keepdims=True)
    kron = dot(tall.astype(F32).astype(BF), p_ref[...]).astype(BF)
    kron = dot(kron, wide.astype(F32).astype(BF)) * gains
    same = lax.rem(lax.broadcasted_iota(jnp.int32, (256, 256), 0), 8) == lax.rem(
        lax.broadcasted_iota(jnp.int32, (256, 256), 1), 8
    )
    return jnp.where(same, kron, 0.0).astype(BF)


def pack_kernel(
    at_ref, w_hbm, p_ref, g_hbm, _, o_ref, k_ref, w_ref, gain_ref, sem, gain_sem
):
    block = pl.multiple_of(at_ref[0] // 128 * 128, 128)
    gains = pltpu.make_async_copy(g_hbm.at[:, pl.ds(block, 128)], gain_ref, gain_sem)
    gains.start()
    slots = w_ref.shape[0]

    def copy(i):
        slot = lax.rem(i, slots)
        return pltpu.make_async_copy(w_hbm.at[:, pl.ds(2 * i, 2)], w_ref.at[slot], sem.at[slot])

    for i in range(slots - 1):
        copy(i).start()

    gains.wait()
    k_ref[...] = kron_operand(at_ref[0], p_ref, gain_ref)

    def one(i, carry):
        @pl.when(i + slots - 1 < M)
        def _():
            copy(i + slots - 1).start()

        copy(i).wait()
        slot = lax.rem(i, slots)
        for part in range(2):
            o_ref[part, i] = jnp.concatenate(
                [w_ref[slot, part, 0], w_ref[slot, part, 1]], axis=-1
            )
        return carry

    lax.fori_loop(0, M, one, 0)


def pack_weight(bias_index, weight, pointwise_weight, gain_table, first):
    return pl.pallas_call(
        pack_kernel,
        in_specs=[SMEM, HBM, VMEM, HBM, UNREAD],
        out_specs=[VMEM, VMEM],
        out_shape=[
            pltpu.VMEM((2, M, 32, 32, 128), BF),
            jax.ShapeDtypeStruct((256, 256), BF),
        ],
        scratch_shapes=[
            pltpu.VMEM((9, 2, 2, 32, 32, 64), BF),
            pltpu.VMEM((32, 128), BF),
            pltpu.SemaphoreType.DMA((9,)),
            pltpu.SemaphoreType.DMA(()),
        ],
        compiler_params=params(16),
        cost_estimate=cost(8),
        name="pack_weight",
    )(bias_index, in_hbm(weight), pointwise_weight, in_hbm(gain_table.T), first)


def back_modes_kernel(
    me_ref, r0, r1, r2, r3, other_ref, x_hbm, w_ref, spread_hbm, g_ref, o_ref,
    x_ref, spread_ref, sem, g_s, b_s, t_s,
):
    copies = [
        pltpu.make_async_copy(x_hbm.at[me_ref[0]], x_ref, sem.at[0]),
        pltpu.make_async_copy(spread_hbm, spread_ref, sem.at[1]),
    ]
    for copy in copies:
        copy.start()

    def store(c, value):
        for co in range(4):
            cut = value[co * 32 : co * 32 + 32]
            g_ref[co * 8 + c] = cut.astype(BF)
            g_s[pl.ds((co * 8 + c) * 32, 32), :] = cut

    copies[0].wait()
    axial_modes(
        x_ref[...], (r0, r1, r2, r3), other_ref, spread_ref, copies[1].wait, True, store
    )

    def line(i, carry):
        g_re = g_s[pl.ds(i, 32, stride=32), :]
        g_im = g_s[pl.ds(i + 16, 32, stride=32), :]
        for c in range(32):
            w_re = w_ref[0, i, c].astype(F32)
            w_im = w_ref[1, i, c].astype(F32)
            re = w_re * g_re + w_im * g_im
            im = w_re * g_im - w_im * g_re
            t_s[0, c * 8 : c * 8 + 8, :] = (re[:8] + re[8:16]) + (re[16:24] + re[24:])
            t_s[1, c * 8 : c * 8 + 8, :] = (im[:8] + im[8:16]) + (im[16:24] + im[24:])
        for part in range(2):
            total = t_s[part, pl.ds(0, 32, stride=8), :]
            for k in range(1, 8):
                total = total + t_s[part, pl.ds(k, 32, stride=8), :]
            b_s[pl.ds(pl.multiple_of((part * 16 + i) * 32, 32), 32), :] = total * ORTHO
        return carry

    lax.fori_loop(0, M, line, 0)
    low = lax.broadcasted_iota(jnp.int32, (32, 128), 1) < 64
    stacks = [[], []]
    for co in range(4):
        cuts = [b_s[pl.ds(co * 8 + c, 32, stride=32), :] for c in range(8)]
        for a2 in range(2):
            keep = low if a2 == 0 else jnp.logical_not(low)
            stacks[a2].append(
                jnp.concatenate([jnp.where(keep, cut, 0.0).astype(BF) for cut in cuts], axis=1)
            )
    moved = lax.dot_general(
        jnp.concatenate(stacks[0] + stacks[1], axis=0),
        spread_ref[...],
        (((1,), (1,)), ((), ())),
        preferred_element_type=F32,
    ).astype(BF)
    for a2 in range(2):
        for co in range(4):
            at = (a2 * 4 + co) * 32
            o_ref[a2 * 32 : a2 * 32 + 32, co * 512 : co * 512 + 512] = moved[at : at + 32]


def back_modes(me, received, other, packed, ops):
    return pl.pallas_call(
        back_modes_kernel,
        in_specs=[SMEM] + [VMEM] * 5 + [HBM, VMEM, HBM],
        out_specs=[VMEM, VMEM],
        out_shape=[
            jax.ShapeDtypeStruct((32, 32, 128), BF),
            jax.ShapeDtypeStruct((64, 2048), BF),
        ],
        scratch_shapes=MODE_SCRATCH
        + [
            pltpu.VMEM((1024, 128), F32),
            pltpu.VMEM((1024, 128), F32),
            pltpu.VMEM((2, 256, 128), F32),
        ],
        compiler_params=params(10),
        cost_estimate=cost(6),
        name="back_modes",
    )(me, *received, other, in_hbm(ops["x"]), in_vmem(packed), in_hbm(ops["spread"]))


def planes_kernel(me_ref, b_ref, x_hbm, *rest):
    outs, (x_ref, sem) = rest[-6:-2], rest[-2:]
    copy = pltpu.make_async_copy(x_hbm.at[me_ref[0]], x_ref, sem)
    copy.start()
    copy.wait()
    table = x_ref[...].astype(F32).T.astype(BF)
    for co in range(4):
        planes = dot(table, b_ref[:, pl.ds(co * 512, 512)]).astype(BF)
        for part in range(2):
            for b in range(4):
                lane = (b * 2 + part) * 512 + co * 128
                for q in range(4):
                    outs[q][:, lane : lane + 128] = planes[
                        part * 64 + q * 16 : part * 64 + q * 16 + 16, b * 128 : b * 128 + 128
                    ]


def back_planes(me, modes, ops, first, name, ahead=()):
    return pl.pallas_call(
        planes_kernel,
        in_specs=[SMEM, VMEM, HBM, UNREAD] + [UNREAD] * len(ahead),
        out_specs=[UNREAD] + [VMEM] * 4,
        out_shape=[jax.ShapeDtypeStruct(first.shape, first.dtype)]
        + [jax.ShapeDtypeStruct((16, 4096), BF)] * 4,
        input_output_aliases={3: 0},
        scratch_shapes=[pltpu.VMEM((64, NX), BF), pltpu.SemaphoreType.DMA(())],
        compiler_params=params(16),
        cost_estimate=cost(1),
        name=name,
    )(me, modes, in_hbm(ops["x"]), first, *ahead)


def weight_grad_kernel(half_ref, u0_ref, u1_ref, g0_ref, g1_ref, o_ref, u_s, g_s):
    i = pl.program_id(0)
    lines = o_ref.shape[1] // 2

    @pl.when(i == 0)
    def _():
        for s, (u, g) in enumerate(((u0_ref, g0_ref), (u1_ref, g1_ref))):
            u_s[s] = u[...].reshape(1024, 128).astype(F32)
            g_s[s] = g[...].reshape(1024, 128).astype(F32)

    base = half_ref[0] * 512
    for k in range(lines):
        at = i * lines + k
        u = [[u_s[s, pl.ds(at + 16 * r, 32, stride=32), :] for r in range(2)] for s in range(2)]
        g = [
            [g_s[s, pl.ds(base + at + 16 * r, 16, stride=32), :] for r in range(2)]
            for s in range(2)
        ]
        for c in range(32):
            row = [
                [jnp.broadcast_to(u[s][r][c : c + 1], (16, 128)) for r in range(2)]
                for s in range(2)
            ]
            re = (row[0][0] * g[0][0] + row[0][1] * g[0][1]) + (
                row[1][0] * g[1][0] + row[1][1] * g[1][1]
            )
            im = (row[0][0] * g[0][1] - row[0][1] * g[0][0]) + (
                row[1][0] * g[1][1] - row[1][1] * g[1][0]
            )
            o_ref[0, 2 * k, c] = re[:, :64]
            o_ref[0, 2 * k + 1, c] = re[:, 64:]
            o_ref[1, 2 * k, c] = im[:, :64]
            o_ref[1, 2 * k + 1, c] = im[:, 64:]


def weight_grad(half, u0, u1, g0, g1):
    return pl.pallas_call(
        weight_grad_kernel,
        grid=(8,),
        in_specs=[SMEM] + [VMEM] * 4,
        out_specs=pl.BlockSpec((2, 4, 32, 16, 64), lambda i: (0, i, 0, 0, 0)),
        scratch_shapes=[pltpu.VMEM((2, 1024, 128), F32), pltpu.VMEM((2, 1024, 128), F32)],
        out_shape=jax.ShapeDtypeStruct((2, 32, 32, 16, 64), F32),
        compiler_params=params(16),
        cost_estimate=cost(8),
        name="weight_grad",
    )(half, u0, u1, g0, g1)


def finish_kernel(
    me_ref, n0, n1, n2, n3, f0, f1, f2, f3, v_ref, k_hbm, y_hbm, z_hbm, o_ref,
    s_ref, a_ref, i_ref, b_ref, k_ref, yt_ref, y_ref, z_ref, in_sem, out_sem, sem,
):
    received = ((n0, n1, n2, n3), (f0, f1, f2, f3))
    nx = o_ref.shape[0]
    slots = b_ref.shape[0]

    def load(x):
        slot = lax.rem(x, slots)
        return pltpu.make_async_copy(v_ref.at[x], i_ref.at[slot], in_sem.at[slot])

    def save(x):
        slot = lax.rem(x, slots)
        return pltpu.make_async_copy(b_ref.at[slot], o_ref.at[x], out_sem.at[slot])

    tables = [
        pltpu.make_async_copy(y_hbm.at[me_ref[0]], yt_ref, sem.at[0]),
        pltpu.make_async_copy(z_hbm, z_ref, sem.at[1]),
        pltpu.make_async_copy(k_hbm, k_ref, sem.at[2]),
    ]
    for table in tables:
        table.start()
    for x in range(slots - 1):
        load(x).start()
    for r in range(64):
        q, j, k = r // 16, (r // 8) % 2, r % 8
        for n in range(4):
            s_ref[n, r * 16 : r * 16 + 16, :] = received[j][q][
                :, k * 512 + n * 128 : k * 512 + n * 128 + 128
            ].astype(F32)
    for table in tables:
        table.wait()
    y_ref[...] = yt_ref[...].astype(F32).T.astype(BF)

    def one(x, carry):
        @pl.when(x + slots - 1 < nx)
        def _():
            load(x + slots - 1).start()

        @pl.when(x >= slots)
        def _():
            save(x - slots).wait()

        load(x).wait()
        slot = lax.rem(x, slots)
        planes = jnp.concatenate(
            [s_ref[n, pl.ds(x, 64, stride=16), :].astype(BF) for n in range(4)], axis=1
        )
        rows = dot(y_ref[...], planes).astype(BF)
        lhs = jnp.concatenate(
            [
                jnp.concatenate(
                    [rows[:128, co * 128 : co * 128 + 128], rows[128:, co * 128 : co * 128 + 128]],
                    axis=1,
                )
                for co in range(4)
            ],
            axis=0,
        )
        for n in range(4):
            part = dot(lhs, z_ref[:, n * 256 : n * 256 + 256])
            for co in range(4):
                for j in range(2):
                    a_ref[co * 8 + n * 2 + j] = part[
                        co * 128 : co * 128 + 128, j * 128 : j * 128 + 128
                    ]
        for y in range(8):
            cut = i_ref[slot, :, y * 16 : y * 16 + 16, :].astype(F32)
            rhs = jnp.concatenate(
                [
                    cut[:, :8].reshape(256, 128).astype(BF),
                    cut[:, 8:].reshape(256, 128).astype(BF),
                ],
                axis=1,
            )
            point = dot(k_ref[...], rhs)
            point = jnp.concatenate(
                [point[:, :128].reshape(32, 8, 128), point[:, 128:].reshape(32, 8, 128)], axis=1
            )
            b_ref[slot, :, y * 16 : y * 16 + 16, :] = (
                point + a_ref[:, y * 16 : y * 16 + 16, :]
            ).astype(BF)
        save(x).start()
        return carry

    lax.fori_loop(0, nx, one, 0)
    for x in range(nx - slots, nx):
        save(x).wait()


def finish(me, near, far, cotangent, kron, ops):
    nx = cotangent.shape[0]
    return pl.pallas_call(
        finish_kernel,
        in_specs=[SMEM] + [VMEM] * 8 + [HBM] * 4,
        out_specs=HBM,
        out_shape=jax.ShapeDtypeStruct(cotangent.shape, BF),
        scratch_shapes=[
            pltpu.VMEM((4, nx * 64, 128), F32),
            pltpu.VMEM((32, NY, NZ), F32),
            pltpu.VMEM((4, 32, NY, NZ), BF),
            pltpu.VMEM((4, 32, NY, NZ), BF),
            pltpu.VMEM((256, 256), BF),
            pltpu.VMEM((64, 256), BF),
            pltpu.VMEM((256, 64), BF),
            pltpu.VMEM((256, 1024), BF),
            pltpu.SemaphoreType.DMA((4,)),
            pltpu.SemaphoreType.DMA((4,)),
            pltpu.SemaphoreType.DMA((3,)),
        ],
        compiler_params=params(24),
        cost_estimate=cost(16),
        name="finish",
    )(
        me, *near, *far, in_hbm(cotangent), in_hbm(kron), in_hbm(ops["y"]),
        in_hbm(ops["z_back"]),
    )


ACROSS = [(s, s ^ 4) for s in range(8)]
SWAP = [(0, 1), (1, 0)]


def in_square(blocks):
    return [blocks[0]] + [
        lax.ppermute(blocks[k], "space", [(s, s ^ k) for s in range(8)]) for k in (1, 2, 3)
    ]


def tuned_device(volume, cotangent, spectral_weight, pointwise_weight, gain_table, bias_index):
    ops = fixed_operands()
    nx = volume.shape[1]
    vol = volume.reshape(nx, 32, NY, NZ)
    cot = cotangent.reshape(nx, 32, NY, NZ)
    me = lax.axis_index("space").astype(jnp.int32).reshape(1)
    half = lax.axis_index("dp").astype(jnp.int32).reshape(1)
    weight = jnp.transpose(spectral_weight, (0, 1, 3, 4, 2))

    cot_blocks = lateral(me, cot, ops, me, "cotangent_lateral")
    cot_received = in_square(cot_blocks)
    vol_blocks = lateral(me, vol, ops, cot_blocks[0], "volume_lateral")
    cot_partner, passed = partner_modes(
        me, cot_received, ops, vol_blocks[1], "cotangent_partner"
    )
    other = lax.ppermute(cot_partner, "space", ACROSS)
    vol_received = in_square([vol_blocks[0], passed, vol_blocks[2], vol_blocks[3]])
    packed, kron = pack_weight(bias_index, weight, pointwise_weight, gain_table, cot_partner)
    g_modes, back_own = back_modes(me, cot_received, other, packed, ops)
    back_other = lax.ppermute(back_own, "space", ACROSS)
    vol_partner, _ = partner_modes(me, vol_received, ops, back_own, "volume_partner")
    vol_partner, *own_planes = back_planes(me, back_own, ops, vol_partner, "own_planes")
    back_near = in_square(own_planes)
    vol_partner, *other_planes = back_planes(
        me, back_other, ops, vol_partner, "partner_planes", back_near[1:]
    )
    back_far = in_square(other_planes)
    vol_other = lax.ppermute(vol_partner, "space", ACROSS)
    u_modes = volume_modes(me, vol_received, vol_other, ops, back_far[1:])
    g_other = lax.ppermute(g_modes, "dp", SWAP)
    u_other = lax.ppermute(u_modes, "dp", SWAP)
    grad = weight_grad(half, u_modes, u_other, g_modes, g_other)
    out = finish(me, back_near, back_far, cot, kron, ops)
    return out.reshape(volume.shape), jnp.transpose(grad, (0, 1, 4, 2, 3))


def per_device(volume, cotangent, spectral_weight, pointwise_weight, gain_table, bias_index):
    fits = (
        volume.shape == (1, 16, 32, NY, NZ)
        and spectral_weight.shape == (2, 2 * M, 64, 32, 32)
        and lax.axis_size("space") == 8
        and lax.axis_size("dp") == 2
    )
    device = tuned_device if fits else general_device
    return device(
        volume, cotangent, spectral_weight, pointwise_weight, gain_table, bias_index
    )


def solution(mesh):
    return jax.shard_map(
        per_device,
        mesh=mesh,
        in_specs=(
            P(("parts", "dp"), "space", None, None, None),
            P(("parts", "dp"), "space", None, None, None),
            P(None, None, "space", None, None),
            P(),
            P(),
            P(("parts", "dp")),
        ),
        out_specs=(
            P(("parts", "dp"), "space", None, None, None),
            P("parts", None, "space", None, "dp"),
        ),
        check_vma=False,
    )
```

```python
import functools
import math

import jax
import jax.numpy as jnp
import numpy as np
from jax import lax
from jax.experimental import pallas as pl
from jax.experimental.pallas import tpu as pltpu
from jax.sharding import PartitionSpec as P

M = 16
NX = 128
NY = 128
NZ = 128


def trig_tables(length, modes_count, signed):
    positions = jnp.arange(length, dtype=jnp.int32)
    mode_base = jnp.arange(modes_count, dtype=jnp.int32)
    if signed:
        frequency = jnp.concatenate([mode_base, mode_base - modes_count])
    else:
        frequency = mode_base
    phase_index = jnp.mod(positions[:, None] * frequency[None, :], length)
    angles = phase_index.astype(jnp.float32) * (2.0 * math.pi / length)
    return (jnp.cos(angles).astype(jnp.bfloat16), jnp.sin(angles).astype(jnp.bfloat16))


def general_device(volume, cotangent, spectral_weight, pointwise_weight, gain_table, bias_index):
    cos_z, sin_z = trig_tables(NZ, M, False)
    cos_y, sin_y = trig_tables(NY, M, True)
    cos_x, sin_x = trig_tables(NX, M, True)
    table_z = jnp.concatenate([cos_z, -sin_z], axis=1)
    table_y = jnp.concatenate([cos_y, sin_y], axis=1)
    paired_y = jnp.stack([cos_y, sin_y], axis=1)
    table_x = jnp.concatenate([cos_x, sin_x], axis=1)
    paired_x = jnp.stack([cos_x, sin_x], axis=1)
    ortho_scale = 1.0 / math.sqrt(NX * NY * NZ)
    pair_count = spectral_weight.shape[2]
    global_pairs = lax.axis_index("space") * pair_count + jnp.arange(pair_count, dtype=jnp.int32)
    flat_scale = jnp.full((pair_count,), ortho_scale, dtype=jnp.float32)
    doubled_scale = jnp.where(global_pairs % M == 0, 1.0, 2.0).astype(jnp.float32) * ortho_scale

    def lateral_spectrum(values_in):
        along_z = jnp.einsum(
            "sxcyz,zk->sxcky", values_in, table_z, preferred_element_type=jnp.float32
        ).astype(jnp.bfloat16)
        products = jnp.einsum(
            "sxcky,yj->sxckj", along_z, table_y, preferred_element_type=jnp.float32
        )
        real_part = products[:, :, :, :M, : 2 * M] + products[:, :, :, M:, 2 * M :]
        imag_part = products[:, :, :, M:, : 2 * M] - products[:, :, :, :M, 2 * M :]
        stacked = jnp.swapaxes(jnp.stack([real_part, imag_part], axis=2), 4, 5).astype(jnp.bfloat16)
        return stacked.reshape(stacked.shape[0], stacked.shape[1], 2, stacked.shape[3], 2 * M * M)

    def axial_spectrum(received, pair_scale):
        products = jnp.einsum(
            "sxrcp,xj->srjpc", received, table_x, preferred_element_type=jnp.float32
        )
        real_part = products[:, 0, : 2 * M] + products[:, 1, 2 * M :]
        imag_part = products[:, 1, : 2 * M] - products[:, 0, 2 * M :]
        stacked = jnp.stack([real_part, imag_part], axis=1)
        return (stacked * pair_scale[None, None, None, :, None]).astype(jnp.bfloat16)

    volume_hat = axial_spectrum(
        lax.all_to_all(lateral_spectrum(volume), "space", split_axis=4, concat_axis=1, tiled=True),
        flat_scale,
    )
    cotangent_hat = axial_spectrum(
        lax.all_to_all(
            lateral_spectrum(cotangent), "space", split_axis=4, concat_axis=1, tiled=True
        ),
        doubled_scale,
    )
    grad_real = jnp.einsum(
        "sapc,sapo->apco", volume_hat[:, 0], cotangent_hat[:, 0], preferred_element_type=jnp.float32
    ) + jnp.einsum(
        "sapc,sapo->apco", volume_hat[:, 1], cotangent_hat[:, 1], preferred_element_type=jnp.float32
    )
    grad_imag = jnp.einsum(
        "sapc,sapo->apco", volume_hat[:, 0], cotangent_hat[:, 1], preferred_element_type=jnp.float32
    ) - jnp.einsum(
        "sapc,sapo->apco", volume_hat[:, 1], cotangent_hat[:, 0], preferred_element_type=jnp.float32
    )
    spectral_grad = lax.psum_scatter(
        jnp.stack([grad_real, grad_imag]).astype(jnp.bfloat16),
        "dp",
        scatter_dimension=4,
        tiled=True,
    ).astype(jnp.float32)
    weight_real = spectral_weight[0]
    weight_imag = spectral_weight[1]
    cot_real = cotangent_hat[:, 0]
    cot_imag = cotangent_hat[:, 1]
    back_real = jnp.einsum(
        "apco,sapo->sapc", weight_real, cot_real, preferred_element_type=jnp.float32
    ) + jnp.einsum("apco,sapo->sapc", weight_imag, cot_imag, preferred_element_type=jnp.float32)
    back_imag = jnp.einsum(
        "apco,sapo->sapc", weight_real, cot_imag, preferred_element_type=jnp.float32
    ) - jnp.einsum("apco,sapo->sapc", weight_imag, cot_real, preferred_element_type=jnp.float32)
    back_modes = jnp.stack([back_real, back_imag], axis=1).astype(jnp.bfloat16)
    products = jnp.einsum(
        "srapc,xta->srtxcp", back_modes, paired_x, preferred_element_type=jnp.float32
    )
    plane_real = products[:, 0, 0] - products[:, 1, 1]
    plane_imag = products[:, 0, 1] + products[:, 1, 0]
    back_planes = jnp.stack([plane_real, plane_imag], axis=2).astype(jnp.bfloat16)
    received = lax.all_to_all(back_planes, "space", split_axis=1, concat_axis=4, tiled=True)
    mode_grid = received.reshape(
        received.shape[0], received.shape[1], 2, received.shape[3], 2 * M, M
    )
    row_products = jnp.einsum(
        "nxrcbd,ytb->nxrtcyd", mode_grid, paired_y, preferred_element_type=jnp.float32
    )
    row_real = row_products[:, :, 0, 0] - row_products[:, :, 1, 1]
    row_imag = row_products[:, :, 0, 1] + row_products[:, :, 1, 0]
    row_values = jnp.concatenate([row_real, row_imag], axis=4).astype(jnp.bfloat16)
    spectral_part = (
        jnp.einsum("nxcyk,kz->nxcyz", row_values, table_z.T, preferred_element_type=jnp.float32)
        * ortho_scale
    )
    bias_rows = (
        bias_index[:, None] == jnp.arange(gain_table.shape[0], dtype=jnp.int32)[None, :]
    ).astype(jnp.bfloat16)
    gain_rows = jnp.dot(bias_rows, gain_table, preferred_element_type=jnp.float32)
    scaled = (cotangent * gain_rows[:, None, :, None, None]).astype(jnp.bfloat16)
    pointwise_part = jnp.einsum(
        "co,sxoyz->sxcyz", pointwise_weight, scaled, preferred_element_type=jnp.float32
    )
    return ((spectral_part + pointwise_part).astype(jnp.bfloat16), spectral_grad)


BF = jnp.bfloat16
F32 = jnp.float32
ORTHO = 1.0 / math.sqrt(NX * NY * NZ)


def host_tables(length, modes_count, signed):
    frequency = np.arange(modes_count)
    if signed:
        frequency = np.concatenate([frequency, frequency - modes_count])
    phase = np.mod(np.arange(length)[:, None] * frequency[None, :], length)
    angles = phase.astype(np.float32) * np.float32(2.0 * math.pi / length)
    cos = np.cos(angles).astype(jnp.bfloat16).astype(np.float32)
    sin = np.sin(angles).astype(jnp.bfloat16).astype(np.float32)
    return cos, sin


def fixed_operands():
    cz, sz = host_tables(NZ, M, False)
    cy, sy = host_tables(NY, M, True)
    cx, sx = host_tables(NX, M, True)
    z_ops = np.zeros((8, NZ, 2, 8, M), np.float32)
    for c in range(8):
        z_ops[c, :, 0, c] = cz
        z_ops[c, :, 1, c] = -sz
    z_ops = z_ops.reshape(8 * NZ, 16 * M)
    y_all = np.stack([np.concatenate([cy.T, sy.T], 1), np.concatenate([-sy.T, cy.T], 1)], 1)
    y_all = y_all.reshape(8, 4, 2, 2 * NY)
    x_all = np.stack([np.stack([cx.T, sx.T], 1), np.stack([-sx.T, cx.T], 1)], 0)
    x_all = x_all.reshape(2, M, 2, 2, 8, 16).transpose(2, 0, 1, 3, 4, 5)
    order = [[[s ^ (4 * j + k) for j in range(2)] for k in range(4)] for s in range(8)]
    y_ops = np.stack([y_all[order[s]] for s in range(8)]).reshape(8, 64, 2 * NY)
    x_ops = np.stack([x_all[..., [s ^ k for k in range(4)], :] for s in range(8)])
    x_ops = x_ops.reshape(8, 64, NX)
    shuffle = np.zeros((4, 8, M, 8, 2, 4, M), np.float32)
    for b in range(4):
        for c in range(8):
            for d in range(M):
                shuffle[b, c, d, c, :, b, d] = 1.0
    shuffle = shuffle.reshape(32 * M, 64 * M)
    ops = dict(z_fwd=z_ops, z_back=z_ops.T, y=y_ops, x=x_ops, spread=shuffle)
    return {k: jnp.asarray(np.ascontiguousarray(v).astype(jnp.bfloat16)) for k, v in ops.items()}


def dot(a, b):
    return jnp.dot(a, b, preferred_element_type=F32)


def params(mib):
    return pltpu.CompilerParams(vmem_limit_bytes=mib << 20)


def cost(us, mib=1):
    return pl.CostEstimate(
        flops=int(us * 6e6), bytes_accessed=mib << 10, transcendentals=0
    )


VMEM = pl.BlockSpec(memory_space=pltpu.VMEM)
SMEM = pl.BlockSpec(memory_space=pltpu.SMEM)
HBM = pl.BlockSpec(memory_space=pltpu.HBM)
UNREAD = pl.BlockSpec(memory_space=pl.ANY)


def in_vmem(x):
    return pltpu.with_memory_space_constraint(x, pltpu.VMEM)


def in_hbm(x):
    return pltpu.with_memory_space_constraint(x, pltpu.HBM)


GROUP = 4
SLOTS = 12


def lateral_kernel(me_ref, v_ref, z_hbm, y_hbm, _, *rest):
    outs, (s_ref, z_ref, y_ref, b_ref, sem, z_sem) = rest[:4], rest[4:]
    nx = v_ref.shape[0]

    def copy(x):
        slot = lax.rem(x, SLOTS)
        return pltpu.make_async_copy(v_ref.at[x], b_ref.at[slot], sem.at[slot])

    tables = [
        pltpu.make_async_copy(z_hbm, z_ref, z_sem.at[0]),
        pltpu.make_async_copy(y_hbm.at[me_ref[0]], y_ref, z_sem.at[1]),
    ]
    for x in range(GROUP):
        copy(x).start()
    for table in tables:
        table.start()
    for x in range(GROUP, SLOTS - GROUP):
        copy(x).start()
    for table in tables:
        table.wait()

    def one(i, carry):
        for k in range(GROUP):
            x = i * GROUP + k
            ahead = x + SLOTS - GROUP

            @pl.when(ahead < nx)
            def _():
                copy(ahead).start()

            copy(x).wait()
        rows = [
            jnp.concatenate(
                [b_ref[lax.rem(i * GROUP + k, SLOTS), co * 8 + c] for c in range(8)], axis=1
            )
            for k in range(GROUP)
            for co in range(4)
        ]
        along = dot(jnp.concatenate(rows, axis=0), z_ref[...]).astype(BF)
        for k in range(GROUP):
            for h in range(2):
                at = (k * 2 + h) * 256
                lo = along[at : at + 128]
                hi = along[at + 128 : at + 256]
                rhs = jnp.concatenate(
                    [
                        jnp.concatenate([lo[:, :128], hi[:, :128]], axis=1),
                        jnp.concatenate([lo[:, 128:], hi[:, 128:]], axis=1),
                    ],
                    axis=0,
                )
                out = dot(y_ref[...], rhs)
                for j in range(2):
                    s_ref[h * 2 + j, pl.ds(i * GROUP + k, 64, stride=16), :] = out[
                        :, j * 128 : j * 128 + 128
                    ]
        return carry

    lax.fori_loop(0, nx // GROUP, one, 0)
    for r in range(64):
        q, j, k = r // 16, (r // 8) % 2, r % 8
        for n in range(4):
            cut = s_ref[n, r * 16 : r * 16 + 16, :].astype(BF)
            outs[q][j, :, k * 512 + n * 128 : k * 512 + n * 128 + 128] = cut


def lateral(me, values, ops, first, name):
    nx = values.shape[0]
    return pl.pallas_call(
        lateral_kernel,
        in_specs=[SMEM, HBM, HBM, HBM, UNREAD],
        out_specs=[VMEM] * 4,
        out_shape=[jax.ShapeDtypeStruct((2, nx, 4096), BF)] * 4,
        scratch_shapes=[
            pltpu.VMEM((4, nx * 64, 128), F32),
            pltpu.VMEM((1024, 256), BF),
            pltpu.VMEM((64, 256), BF),
            pltpu.VMEM((SLOTS, 32, NY, NZ), BF),
            pltpu.SemaphoreType.DMA((SLOTS,)),
            pltpu.SemaphoreType.DMA((2,)),
        ],
        compiler_params=params(20),
        cost_estimate=cost(10),
        name=name,
    )(me, in_hbm(values), in_hbm(ops["z_fwd"]), in_hbm(ops["y"]), first)


def square_sum(table, refs, j, b):
    rhs = jnp.concatenate(
        [ref[j, :, pl.ds(b * 1024 + part * 512, 512)] for part in range(2) for ref in refs],
        axis=0,
    )
    return dot(table, rhs)


def partner_kernel(me_ref, r0, r1, r2, r3, x_hbm, _, o_ref, __, x_ref, sem):
    copy = pltpu.make_async_copy(x_hbm.at[me_ref[0]], x_ref, sem)
    copy.start()
    copy.wait()
    for b in range(4):
        o_ref[:, pl.ds(b * 512, 512)] = square_sum(x_ref[...], (r0, r1, r2, r3), 1, b).astype(BF)


def partner_modes(me, received, ops, passed, name):
    return pl.pallas_call(
        partner_kernel,
        in_specs=[SMEM] + [VMEM] * 4 + [HBM, UNREAD],
        out_specs=[VMEM, UNREAD],
        out_shape=[
            jax.ShapeDtypeStruct((64, 2048), BF),
            jax.ShapeDtypeStruct(passed.shape, passed.dtype),
        ],
        input_output_aliases={6: 1},
        scratch_shapes=[pltpu.VMEM((64, NX), BF), pltpu.SemaphoreType.DMA(())],
        compiler_params=params(16),
        cost_estimate=cost(1),
        name=name,
    )(me, *received, in_hbm(ops["x"]), passed)


def axial_modes(table, refs, other_ref, spread_ref, ready, doubled, store):
    lane = lax.broadcasted_iota(jnp.int32, (1, 512), 1)
    scale = jnp.where(lane % M == 0, ORTHO, (2.0 if doubled else 1.0) * ORTHO).astype(F32)
    cuts = [
        (
            (square_sum(table, refs, 0, b) + other_ref[:, pl.ds(b * 512, 512)].astype(F32)) * scale
        ).astype(BF)
        for b in range(4)
    ]
    both = jnp.concatenate(
        [
            jnp.concatenate(
                [cut[a2 * 32 : a2 * 32 + 32, co * 128 : co * 128 + 128] for cut in cuts], axis=1
            )
            for a2 in range(2)
            for co in range(4)
        ],
        axis=0,
    )
    low = lax.broadcasted_iota(jnp.int32, (128, 128), 1) < 64
    ready()
    for c in range(0, 8, 2):
        moved = dot(both, spread_ref[:, pl.ds(c * 128, 256)])
        for k in range(2):
            cut = moved[:, k * 128 : k * 128 + 128]
            store(c + k, jnp.where(low, cut[:128], cut[128:]))


def volume_modes_kernel(
    me_ref, r0, r1, r2, r3, other_ref, x_hbm, spread_hbm, *rest
):
    o_ref, x_ref, spread_ref, sem = rest[-4:]
    copies = [
        pltpu.make_async_copy(x_hbm.at[me_ref[0]], x_ref, sem.at[0]),
        pltpu.make_async_copy(spread_hbm, spread_ref, sem.at[1]),
    ]
    for copy in copies:
        copy.start()

    def store(c, value):
        for co in range(4):
            o_ref[co * 8 + c] = value[co * 32 : co * 32 + 32].astype(BF)

    copies[0].wait()
    axial_modes(
        x_ref[...], (r0, r1, r2, r3), other_ref, spread_ref, copies[1].wait, False, store
    )


MODE_SCRATCH = [
    pltpu.VMEM((64, NX), BF),
    pltpu.VMEM((512, 1024), BF),
    pltpu.SemaphoreType.DMA((2,)),
]


def volume_modes(me, received, other, ops, ahead):
    return pl.pallas_call(
        volume_modes_kernel,
        in_specs=[SMEM] + [VMEM] * 5 + [HBM] * 2 + [HBM] * len(ahead),
        out_specs=VMEM,
        out_shape=jax.ShapeDtypeStruct((32, 32, 128), BF),
        scratch_shapes=MODE_SCRATCH,
        compiler_params=params(16),
        cost_estimate=cost(1.5),
        name="volume_modes",
    )(me, *received, other, in_hbm(ops["x"]), in_hbm(ops["spread"]), *ahead)


def kron_operand(at, p_ref, gain_ref):
    lane = lax.broadcasted_iota(jnp.int32, (32, 128), 1)
    here = lane == lax.rem(at, 128)
    gain = jnp.sum(jnp.where(here, gain_ref[...].astype(F32), 0.0), axis=1, keepdims=True)
    wide = (
        lax.broadcasted_iota(jnp.int32, (32, 256), 0)
        == lax.broadcasted_iota(jnp.int32, (32, 256), 1) // 8
    )
    tall = (
        lax.broadcasted_iota(jnp.int32, (256, 32), 0) // 8
        == lax.broadcasted_iota(jnp.int32, (256, 32), 1)
    )
    gains = jnp.sum(jnp.where(wide, gain, 0.0), axis=0, keepdims=True)
    kron = dot(tall.astype(F32).astype(BF), p_ref[...]).astype(BF)
    kron = dot(kron, wide.astype(F32).astype(BF)) * gains
    same = lax.rem(lax.broadcasted_iota(jnp.int32, (256, 256), 0), 8) == lax.rem(
        lax.broadcasted_iota(jnp.int32, (256, 256), 1), 8
    )
    return jnp.where(same, kron, 0.0).astype(BF)


def pack_kernel(
    at_ref, w_hbm, p_ref, g_hbm, _, o_ref, k_ref, w_ref, gain_ref, sem, gain_sem
):
    block = pl.multiple_of(at_ref[0] // 128 * 128, 128)
    gains = pltpu.make_async_copy(g_hbm.at[:, pl.ds(block, 128)], gain_ref, gain_sem)
    gains.start()
    slots = w_ref.shape[0]

    def copy(i):
        slot = lax.rem(i, slots)
        return pltpu.make_async_copy(w_hbm.at[:, pl.ds(2 * i, 2)], w_ref.at[slot], sem.at[slot])

    for i in range(slots - 1):
        copy(i).start()

    gains.wait()
    k_ref[...] = kron_operand(at_ref[0], p_ref, gain_ref)

    def one(i, carry):
        @pl.when(i + slots - 1 < M)
        def _():
            copy(i + slots - 1).start()

        copy(i).wait()
        slot = lax.rem(i, slots)
        for part in range(2):
            o_ref[part, i] = jnp.concatenate(
                [w_ref[slot, part, 0], w_ref[slot, part, 1]], axis=-1
            )
        return carry

    lax.fori_loop(0, M, one, 0)


def pack_weight(bias_index, weight, pointwise_weight, gain_table, first):
    return pl.pallas_call(
        pack_kernel,
        in_specs=[SMEM, HBM, VMEM, HBM, UNREAD],
        out_specs=[VMEM, VMEM],
        out_shape=[
            pltpu.VMEM((2, M, 32, 32, 128), BF),
            pltpu.HBM((256, 256), BF),
        ],
        scratch_shapes=[
            pltpu.VMEM((9, 2, 2, 32, 32, 64), BF),
            pltpu.VMEM((32, 128), BF),
            pltpu.SemaphoreType.DMA((9,)),
            pltpu.SemaphoreType.DMA(()),
        ],
        compiler_params=params(16),
        cost_estimate=cost(8),
        name="pack_weight",
    )(bias_index, in_hbm(weight), pointwise_weight, in_hbm(gain_table.T), first)


def back_modes_kernel(
    me_ref, r0, r1, r2, r3, other_ref, x_hbm, w_ref, spread_hbm, g_ref, o_ref,
    x_ref, spread_ref, sem, g_s, b_s, t_s,
):
    copies = [
        pltpu.make_async_copy(x_hbm.at[me_ref[0]], x_ref, sem.at[0]),
        pltpu.make_async_copy(spread_hbm, spread_ref, sem.at[1]),
    ]
    for copy in copies:
        copy.start()

    def store(c, value):
        for co in range(4):
            cut = value[co * 32 : co * 32 + 32]
            g_ref[co * 8 + c] = cut.astype(BF)
            g_s[pl.ds((co * 8 + c) * 32, 32), :] = cut

    copies[0].wait()
    axial_modes(
        x_ref[...], (r0, r1, r2, r3), other_ref, spread_ref, copies[1].wait, True, store
    )

    def line(i, carry):
        g_re = g_s[pl.ds(i, 32, stride=32), :]
        g_im = g_s[pl.ds(i + 16, 32, stride=32), :]
        for c in range(32):
            w_re = w_ref[0, i, c].astype(F32)
            w_im = w_ref[1, i, c].astype(F32)
            re = w_re * g_re + w_im * g_im
            im = w_re * g_im - w_im * g_re
            t_s[0, c * 8 : c * 8 + 8, :] = (re[:8] + re[8:16]) + (re[16:24] + re[24:])
            t_s[1, c * 8 : c * 8 + 8, :] = (im[:8] + im[8:16]) + (im[16:24] + im[24:])
        for part in range(2):
            total = t_s[part, pl.ds(0, 32, stride=8), :]
            for k in range(1, 8):
                total = total + t_s[part, pl.ds(k, 32, stride=8), :]
            b_s[pl.ds(pl.multiple_of((part * 16 + i) * 32, 32), 32), :] = total * ORTHO
        return carry

    lax.fori_loop(0, M, line, 0)
    low = lax.broadcasted_iota(jnp.int32, (32, 128), 1) < 64
    stacks = [[], []]
    for co in range(4):
        cuts = [b_s[pl.ds(co * 8 + c, 32, stride=32), :] for c in range(8)]
        for a2 in range(2):
            keep = low if a2 == 0 else jnp.logical_not(low)
            stacks[a2].append(
                jnp.concatenate([jnp.where(keep, cut, 0.0).astype(BF) for cut in cuts], axis=1)
            )
    moved = lax.dot_general(
        jnp.concatenate(stacks[0] + stacks[1], axis=0),
        spread_ref[...],
        (((1,), (1,)), ((), ())),
        preferred_element_type=F32,
    ).astype(BF)
    for a2 in range(2):
        for co in range(4):
            at = (a2 * 4 + co) * 32
            o_ref[a2 * 32 : a2 * 32 + 32, co * 512 : co * 512 + 512] = moved[at : at + 32]


def back_modes(me, received, other, packed, ops):
    return pl.pallas_call(
        back_modes_kernel,
        in_specs=[SMEM] + [VMEM] * 5 + [HBM, VMEM, HBM],
        out_specs=[VMEM, VMEM],
        out_shape=[
            jax.ShapeDtypeStruct((32, 32, 128), BF),
            jax.ShapeDtypeStruct((64, 2048), BF),
        ],
        scratch_shapes=MODE_SCRATCH
        + [
            pltpu.VMEM((1024, 128), F32),
            pltpu.VMEM((1024, 128), F32),
            pltpu.VMEM((2, 256, 128), F32),
        ],
        compiler_params=params(10),
        cost_estimate=cost(6),
        name="back_modes",
    )(me, *received, other, in_hbm(ops["x"]), in_vmem(packed), in_hbm(ops["spread"]))


def planes_kernel(me_ref, b_ref, x_hbm, *rest):
    outs, (x_ref, sem) = rest[-6:-2], rest[-2:]
    copy = pltpu.make_async_copy(x_hbm.at[me_ref[0]], x_ref, sem)
    copy.start()
    copy.wait()
    table = x_ref[...].astype(F32).T.astype(BF)
    for co in range(4):
        planes = dot(table, b_ref[:, pl.ds(co * 512, 512)]).astype(BF)
        for part in range(2):
            for b in range(4):
                lane = (b * 2 + part) * 512 + co * 128
                for q in range(4):
                    outs[q][:, lane : lane + 128] = planes[
                        part * 64 + q * 16 : part * 64 + q * 16 + 16, b * 128 : b * 128 + 128
                    ]


def back_planes(me, modes, ops, first, name, ahead=(), far=()):
    return pl.pallas_call(
        planes_kernel,
        in_specs=[SMEM, VMEM, HBM, UNREAD] + [UNREAD] * len(ahead) + [HBM] * len(far),
        out_specs=[UNREAD] + [VMEM] * 4,
        out_shape=[jax.ShapeDtypeStruct(first.shape, first.dtype)]
        + [jax.ShapeDtypeStruct((16, 4096), BF)] * 4,
        input_output_aliases={3: 0},
        scratch_shapes=[pltpu.VMEM((64, NX), BF), pltpu.SemaphoreType.DMA(())],
        compiler_params=params(16),
        cost_estimate=cost(1),
        name=name,
    )(me, modes, in_hbm(ops["x"]), first, *ahead, *[in_hbm(x) for x in far])


def weight_grad_kernel(half_ref, u0_ref, u1_ref, g0_ref, g1_ref, o_ref, u_s, g_s):
    i = pl.program_id(0)
    lines = o_ref.shape[1] // 2

    @pl.when(i == 0)
    def _():
        for s, (u, g) in enumerate(((u0_ref, g0_ref), (u1_ref, g1_ref))):
            u_s[s] = u[...].reshape(1024, 128).astype(F32)
            g_s[s] = g[...].reshape(1024, 128).astype(F32)

    base = half_ref[0] * 512
    for k in range(lines):
        at = i * lines + k
        u = [[u_s[s, pl.ds(at + 16 * r, 32, stride=32), :] for r in range(2)] for s in range(2)]
        g = [
            [g_s[s, pl.ds(base + at + 16 * r, 16, stride=32), :] for r in range(2)]
            for s in range(2)
        ]
        for c in range(32):
            row = [
                [jnp.broadcast_to(u[s][r][c : c + 1], (16, 128)) for r in range(2)]
                for s in range(2)
            ]
            re = (row[0][0] * g[0][0] + row[0][1] * g[0][1]) + (
                row[1][0] * g[1][0] + row[1][1] * g[1][1]
            )
            im = (row[0][0] * g[0][1] - row[0][1] * g[0][0]) + (
                row[1][0] * g[1][1] - row[1][1] * g[1][0]
            )
            o_ref[0, 2 * k, c] = re[:, :64]
            o_ref[0, 2 * k + 1, c] = re[:, 64:]
            o_ref[1, 2 * k, c] = im[:, :64]
            o_ref[1, 2 * k + 1, c] = im[:, 64:]


def weight_grad(half, u0, u1, g0, g1):
    return pl.pallas_call(
        weight_grad_kernel,
        grid=(4,),
        in_specs=[SMEM] + [VMEM] * 4,
        out_specs=pl.BlockSpec((2, 8, 32, 16, 64), lambda i: (0, i, 0, 0, 0)),
        scratch_shapes=[pltpu.VMEM((2, 1024, 128), F32), pltpu.VMEM((2, 1024, 128), F32)],
        out_shape=jax.ShapeDtypeStruct((2, 32, 32, 16, 64), F32),
        compiler_params=params(16),
        cost_estimate=cost(8),
        name="weight_grad",
    )(half, u0, u1, g0, g1)


def pointwise_kernel(base, v_ref, k_hbm, _, o_ref, __, k_ref, i_ref, in_sem, k_sem):
    nx = o_ref.shape[0]
    slots = i_ref.shape[0]

    def load(x):
        slot = lax.rem(x, slots)
        return pltpu.make_async_copy(v_ref.at[base + x], i_ref.at[slot], in_sem.at[slot])

    table = pltpu.make_async_copy(k_hbm, k_ref, k_sem)
    table.start()
    for x in range(slots - 1):
        load(x).start()
    table.wait()

    def one(x, carry):
        @pl.when(x + slots - 1 < nx)
        def _():
            load(x + slots - 1).start()

        load(x).wait()
        slot = lax.rem(x, slots)
        for y in range(8):
            cut = i_ref[slot, :, y * 16 : y * 16 + 16, :].astype(F32)
            rhs = jnp.concatenate(
                [
                    cut[:, :8].reshape(256, 128).astype(BF),
                    cut[:, 8:].reshape(256, 128).astype(BF),
                ],
                axis=1,
            )
            point = dot(k_ref[...], rhs)
            o_ref[x, :, y * 16 : y * 16 + 16, :] = jnp.concatenate(
                [point[:, :128].reshape(32, 8, 128), point[:, 128:].reshape(32, 8, 128)], axis=1
            ).astype(BF)
        return carry

    lax.fori_loop(0, nx, one, 0)


def pointwise_save_kernel(base, v_ref, k_hbm, _, o_hbm, __, b_ref, out_sem, *scratch):
    k_ref, i_ref, in_sem, k_sem = scratch
    nx = o_hbm.shape[0]
    slots = i_ref.shape[0]

    def load(x):
        slot = lax.rem(x, slots)
        return pltpu.make_async_copy(v_ref.at[base + x], i_ref.at[slot], in_sem.at[slot])

    def save(x):
        slot = lax.rem(x, slots)
        return pltpu.make_async_copy(b_ref.at[slot], o_hbm.at[x], out_sem.at[slot])

    table = pltpu.make_async_copy(k_hbm, k_ref, k_sem)
    table.start()
    for x in range(slots - 1):
        load(x).start()
    table.wait()

    def one(x, carry):
        @pl.when(x + slots - 1 < nx)
        def _():
            load(x + slots - 1).start()

        @pl.when(x >= slots)
        def _():
            save(x - slots).wait()

        load(x).wait()
        slot = lax.rem(x, slots)
        for y in range(8):
            cut = i_ref[slot, :, y * 16 : y * 16 + 16, :].astype(F32)
            rhs = jnp.concatenate(
                [
                    cut[:, :8].reshape(256, 128).astype(BF),
                    cut[:, 8:].reshape(256, 128).astype(BF),
                ],
                axis=1,
            )
            point = dot(k_ref[...], rhs)
            b_ref[slot, :, y * 16 : y * 16 + 16, :] = jnp.concatenate(
                [point[:, :128].reshape(32, 8, 128), point[:, 128:].reshape(32, 8, 128)], axis=1
            ).astype(BF)
        save(x).start()
        return carry

    lax.fori_loop(0, nx, one, 0)
    for x in range(nx - slots, nx):
        save(x).wait()


def pointwise(cotangent, kron, base, count, first, keep, name):
    shape = (count, 32, NY, NZ)
    scratch = [
        pltpu.VMEM((256, 256), BF),
        pltpu.VMEM((4, 32, NY, NZ), BF),
        pltpu.SemaphoreType.DMA((4,)),
        pltpu.SemaphoreType.DMA(()),
    ]
    if not keep:
        scratch = [pltpu.VMEM((4, 32, NY, NZ), BF), pltpu.SemaphoreType.DMA((4,))] + scratch
    return pl.pallas_call(
        functools.partial(pointwise_kernel if keep else pointwise_save_kernel, base),
        in_specs=[HBM, HBM, UNREAD],
        out_specs=[VMEM if keep else HBM, UNREAD],
        out_shape=[
            pltpu.VMEM(shape, BF) if keep else pltpu.HBM(shape, BF),
            jax.ShapeDtypeStruct(first.shape, first.dtype),
        ],
        input_output_aliases={2: 1},
        scratch_shapes=scratch,
        compiler_params=params(12),
        cost_estimate=cost(5),
        name=name,
    )(in_hbm(cotangent), in_hbm(kron), first)


def finish_kernel(
    me_ref, n0, n1, n2, n3, f0, f1, f2, f3, p_ref, q_ref, y_hbm, z_hbm, o_ref,
    s_ref, i_ref, b_ref, yt_ref, y_ref, z_ref, in_sem, out_sem, sem,
):
    received = ((n0, n1, n2, n3), (f0, f1, f2, f3))
    split = p_ref.shape[0]
    total = o_ref.shape[0]
    slots = b_ref.shape[0]

    def load(x):
        slot = lax.rem(x, i_ref.shape[0])
        return pltpu.make_async_copy(p_ref.at[x], i_ref.at[slot], in_sem.at[slot])

    def place(t):
        return lax.rem(t + split, total)

    def save(t):
        slot = lax.rem(t, slots)
        return pltpu.make_async_copy(b_ref.at[slot], o_ref.at[place(t)], out_sem.at[slot])

    tables = [
        pltpu.make_async_copy(y_hbm.at[me_ref[0]], yt_ref, sem.at[0]),
        pltpu.make_async_copy(z_hbm, z_ref, sem.at[1]),
    ]
    for table in tables:
        table.start()
    for r in range(64):
        q, j, k = r // 16, (r // 8) % 2, r % 8
        for n in range(4):
            s_ref[n, r * 16 : r * 16 + 16, :] = received[j][q][
                :, k * 512 + n * 128 : k * 512 + n * 128 + 128
            ].astype(F32)
    for table in tables:
        table.wait()
    y_ref[...] = yt_ref[...].astype(F32).T.astype(BF)
    for x in range(i_ref.shape[0]):
        load(x).start()

    def step(t, point):
        @pl.when(t >= slots)
        def _():
            save(t - slots).wait()

        x = place(t)
        slot = lax.rem(t, slots)
        planes = jnp.concatenate(
            [s_ref[n, pl.ds(x, 64, stride=16), :].astype(BF) for n in range(4)], axis=1
        )
        rows = dot(y_ref[...], planes).astype(BF)
        lhs = jnp.concatenate(
            [
                jnp.concatenate(
                    [rows[:128, co * 128 : co * 128 + 128], rows[128:, co * 128 : co * 128 + 128]],
                    axis=1,
                )
                for co in range(4)
            ],
            axis=0,
        )
        for n in range(4):
            part = dot(lhs, z_ref[:, n * 256 : n * 256 + 256])
            for co in range(4):
                for j in range(2):
                    c = co * 8 + n * 2 + j
                    b_ref[slot, c] = (
                        part[co * 128 : co * 128 + 128, j * 128 : j * 128 + 128]
                        + point[c].astype(F32)
                    ).astype(BF)
        save(t).start()

    def kept(t, carry):
        step(t, q_ref.at[t])
        return carry

    def loaded(x, carry):
        load(x).wait()
        step(x + total - split, i_ref.at[lax.rem(x, i_ref.shape[0])])

        @pl.when(x + i_ref.shape[0] < split)
        def _():
            load(x + i_ref.shape[0]).start()

        return carry

    lax.fori_loop(0, total - split, kept, 0)
    lax.fori_loop(0, split, loaded, 0)
    for t in range(total - slots, total):
        save(t).wait()


def finish(me, near, far, saved, kept, ops):
    nx = saved.shape[0] + kept.shape[0]
    shape = (nx,) + saved.shape[1:]
    return pl.pallas_call(
        finish_kernel,
        in_specs=[SMEM] + [VMEM] * 8 + [HBM, VMEM, HBM, HBM],
        out_specs=HBM,
        out_shape=jax.ShapeDtypeStruct(shape, BF),
        scratch_shapes=[
            pltpu.VMEM((4, nx * 64, 128), F32),
            pltpu.VMEM((4, 32, NY, NZ), BF),
            pltpu.VMEM((4, 32, NY, NZ), BF),
            pltpu.VMEM((64, 256), BF),
            pltpu.VMEM((256, 64), BF),
            pltpu.VMEM((256, 1024), BF),
            pltpu.SemaphoreType.DMA((4,)),
            pltpu.SemaphoreType.DMA((4,)),
            pltpu.SemaphoreType.DMA((2,)),
        ],
        compiler_params=params(16),
        cost_estimate=cost(12),
        name="finish",
    )(
        me, *near, *far, in_hbm(saved), in_vmem(kept), in_hbm(ops["y"]), in_hbm(ops["z_back"])
    )


ACROSS = [(s, s ^ 4) for s in range(8)]
SWAP = [(0, 1), (1, 0)]


def in_square(blocks):
    return [blocks[0]] + [
        lax.ppermute(blocks[k], "space", [(s, s ^ k) for s in range(8)]) for k in (1, 2, 3)
    ]


def tuned_device(volume, cotangent, spectral_weight, pointwise_weight, gain_table, bias_index):
    ops = fixed_operands()
    nx = volume.shape[1]
    vol = volume.reshape(nx, 32, NY, NZ)
    cot = cotangent.reshape(nx, 32, NY, NZ)
    me = lax.axis_index("space").astype(jnp.int32).reshape(1)
    half = lax.axis_index("dp").astype(jnp.int32).reshape(1)
    weight = jnp.transpose(spectral_weight, (0, 1, 3, 4, 2))

    cot_blocks = lateral(me, cot, ops, me, "cotangent_lateral")
    cot_received = in_square(cot_blocks)
    vol_blocks = lateral(me, vol, ops, cot_blocks[0], "volume_lateral")
    cot_partner, passed = partner_modes(
        me, cot_received, ops, vol_blocks[1], "cotangent_partner"
    )
    other = lax.ppermute(cot_partner, "space", ACROSS)
    vol_received = in_square([vol_blocks[0], passed, vol_blocks[2], vol_blocks[3]])
    packed, kron = pack_weight(bias_index, weight, pointwise_weight, gain_table, cot_partner)
    g_modes, back_own = back_modes(me, cot_received, other, packed, ops)
    back_other = lax.ppermute(back_own, "space", ACROSS)
    vol_partner, _ = partner_modes(me, vol_received, ops, back_own, "volume_partner")
    vol_partner, *own_planes = back_planes(me, back_own, ops, vol_partner, "own_planes")
    back_near = in_square(own_planes)
    saved, back_near[0] = pointwise(
        cot, kron, 0, nx // 2, own_planes[0], False, "pointwise_first"
    )
    vol_partner, *other_planes = back_planes(
        me, back_other, ops, vol_partner, "partner_planes", back_near[1:], [saved]
    )
    back_far = in_square(other_planes)
    kept, back_far[0] = pointwise(
        cot, kron, nx // 2, nx - nx // 2, other_planes[0], True, "pointwise_second"
    )
    vol_other = lax.ppermute(vol_partner, "space", ACROSS)
    out = finish(me, back_near, back_far, saved, kept, ops)
    u_modes = volume_modes(me, vol_received, vol_other, ops, [in_hbm(out)])
    g_other = lax.ppermute(g_modes, "dp", SWAP)
    u_other = lax.ppermute(u_modes, "dp", SWAP)
    grad = weight_grad(half, u_modes, u_other, g_modes, g_other)
    return out.reshape(volume.shape), jnp.transpose(grad, (0, 1, 4, 2, 3))


def per_device(volume, cotangent, spectral_weight, pointwise_weight, gain_table, bias_index):
    fits = (
        volume.shape == (1, 16, 32, NY, NZ)
        and spectral_weight.shape == (2, 2 * M, 64, 32, 32)
        and lax.axis_size("space") == 8
        and lax.axis_size("dp") == 2
    )
    device = tuned_device if fits else general_device
    return device(
        volume, cotangent, spectral_weight, pointwise_weight, gain_table, bias_index
    )


def solution(mesh):
    return jax.shard_map(
        per_device,
        mesh=mesh,
        in_specs=(
            P(("parts", "dp"), "space", None, None, None),
            P(("parts", "dp"), "space", None, None, None),
            P(None, None, "space", None, None),
            P(),
            P(),
            P(("parts", "dp")),
        ),
        out_specs=(
            P(("parts", "dp"), "space", None, None, None),
            P("parts", None, "space", None, "dp"),
        ),
        check_vma=False,
    )
```

```python
import functools
import math

import jax
import jax.numpy as jnp
import numpy as np
from jax import lax
from jax.experimental import pallas as pl
from jax.experimental.pallas import tpu as pltpu
from jax.sharding import PartitionSpec as P

M = 16
NX = 128
NY = 128
NZ = 128


def trig_tables(length, modes_count, signed):
    positions = jnp.arange(length, dtype=jnp.int32)
    mode_base = jnp.arange(modes_count, dtype=jnp.int32)
    if signed:
        frequency = jnp.concatenate([mode_base, mode_base - modes_count])
    else:
        frequency = mode_base
    phase_index = jnp.mod(positions[:, None] * frequency[None, :], length)
    angles = phase_index.astype(jnp.float32) * (2.0 * math.pi / length)
    return (jnp.cos(angles).astype(jnp.bfloat16), jnp.sin(angles).astype(jnp.bfloat16))


def general_device(volume, cotangent, spectral_weight, pointwise_weight, gain_table, bias_index):
    cos_z, sin_z = trig_tables(NZ, M, False)
    cos_y, sin_y = trig_tables(NY, M, True)
    cos_x, sin_x = trig_tables(NX, M, True)
    table_z = jnp.concatenate([cos_z, -sin_z], axis=1)
    table_y = jnp.concatenate([cos_y, sin_y], axis=1)
    paired_y = jnp.stack([cos_y, sin_y], axis=1)
    table_x = jnp.concatenate([cos_x, sin_x], axis=1)
    paired_x = jnp.stack([cos_x, sin_x], axis=1)
    ortho_scale = 1.0 / math.sqrt(NX * NY * NZ)
    pair_count = spectral_weight.shape[2]
    global_pairs = lax.axis_index("space") * pair_count + jnp.arange(pair_count, dtype=jnp.int32)
    flat_scale = jnp.full((pair_count,), ortho_scale, dtype=jnp.float32)
    doubled_scale = jnp.where(global_pairs % M == 0, 1.0, 2.0).astype(jnp.float32) * ortho_scale

    def lateral_spectrum(values_in):
        along_z = jnp.einsum(
            "sxcyz,zk->sxcky", values_in, table_z, preferred_element_type=jnp.float32
        ).astype(jnp.bfloat16)
        products = jnp.einsum(
            "sxcky,yj->sxckj", along_z, table_y, preferred_element_type=jnp.float32
        )
        real_part = products[:, :, :, :M, : 2 * M] + products[:, :, :, M:, 2 * M :]
        imag_part = products[:, :, :, M:, : 2 * M] - products[:, :, :, :M, 2 * M :]
        stacked = jnp.swapaxes(jnp.stack([real_part, imag_part], axis=2), 4, 5).astype(jnp.bfloat16)
        return stacked.reshape(stacked.shape[0], stacked.shape[1], 2, stacked.shape[3], 2 * M * M)

    def axial_spectrum(received, pair_scale):
        products = jnp.einsum(
            "sxrcp,xj->srjpc", received, table_x, preferred_element_type=jnp.float32
        )
        real_part = products[:, 0, : 2 * M] + products[:, 1, 2 * M :]
        imag_part = products[:, 1, : 2 * M] - products[:, 0, 2 * M :]
        stacked = jnp.stack([real_part, imag_part], axis=1)
        return (stacked * pair_scale[None, None, None, :, None]).astype(jnp.bfloat16)

    volume_hat = axial_spectrum(
        lax.all_to_all(lateral_spectrum(volume), "space", split_axis=4, concat_axis=1, tiled=True),
        flat_scale,
    )
    cotangent_hat = axial_spectrum(
        lax.all_to_all(
            lateral_spectrum(cotangent), "space", split_axis=4, concat_axis=1, tiled=True
        ),
        doubled_scale,
    )
    grad_real = jnp.einsum(
        "sapc,sapo->apco", volume_hat[:, 0], cotangent_hat[:, 0], preferred_element_type=jnp.float32
    ) + jnp.einsum(
        "sapc,sapo->apco", volume_hat[:, 1], cotangent_hat[:, 1], preferred_element_type=jnp.float32
    )
    grad_imag = jnp.einsum(
        "sapc,sapo->apco", volume_hat[:, 0], cotangent_hat[:, 1], preferred_element_type=jnp.float32
    ) - jnp.einsum(
        "sapc,sapo->apco", volume_hat[:, 1], cotangent_hat[:, 0], preferred_element_type=jnp.float32
    )
    spectral_grad = lax.psum_scatter(
        jnp.stack([grad_real, grad_imag]).astype(jnp.bfloat16),
        "dp",
        scatter_dimension=4,
        tiled=True,
    ).astype(jnp.float32)
    weight_real = spectral_weight[0]
    weight_imag = spectral_weight[1]
    cot_real = cotangent_hat[:, 0]
    cot_imag = cotangent_hat[:, 1]
    back_real = jnp.einsum(
        "apco,sapo->sapc", weight_real, cot_real, preferred_element_type=jnp.float32
    ) + jnp.einsum("apco,sapo->sapc", weight_imag, cot_imag, preferred_element_type=jnp.float32)
    back_imag = jnp.einsum(
        "apco,sapo->sapc", weight_real, cot_imag, preferred_element_type=jnp.float32
    ) - jnp.einsum("apco,sapo->sapc", weight_imag, cot_real, preferred_element_type=jnp.float32)
    back_modes = jnp.stack([back_real, back_imag], axis=1).astype(jnp.bfloat16)
    products = jnp.einsum(
        "srapc,xta->srtxcp", back_modes, paired_x, preferred_element_type=jnp.float32
    )
    plane_real = products[:, 0, 0] - products[:, 1, 1]
    plane_imag = products[:, 0, 1] + products[:, 1, 0]
    back_planes = jnp.stack([plane_real, plane_imag], axis=2).astype(jnp.bfloat16)
    received = lax.all_to_all(back_planes, "space", split_axis=1, concat_axis=4, tiled=True)
    mode_grid = received.reshape(
        received.shape[0], received.shape[1], 2, received.shape[3], 2 * M, M
    )
    row_products = jnp.einsum(
        "nxrcbd,ytb->nxrtcyd", mode_grid, paired_y, preferred_element_type=jnp.float32
    )
    row_real = row_products[:, :, 0, 0] - row_products[:, :, 1, 1]
    row_imag = row_products[:, :, 0, 1] + row_products[:, :, 1, 0]
    row_values = jnp.concatenate([row_real, row_imag], axis=4).astype(jnp.bfloat16)
    spectral_part = (
        jnp.einsum("nxcyk,kz->nxcyz", row_values, table_z.T, preferred_element_type=jnp.float32)
        * ortho_scale
    )
    bias_rows = (
        bias_index[:, None] == jnp.arange(gain_table.shape[0], dtype=jnp.int32)[None, :]
    ).astype(jnp.bfloat16)
    gain_rows = jnp.dot(bias_rows, gain_table, preferred_element_type=jnp.float32)
    scaled = (cotangent * gain_rows[:, None, :, None, None]).astype(jnp.bfloat16)
    pointwise_part = jnp.einsum(
        "co,sxoyz->sxcyz", pointwise_weight, scaled, preferred_element_type=jnp.float32
    )
    return ((spectral_part + pointwise_part).astype(jnp.bfloat16), spectral_grad)


BF = jnp.bfloat16
F32 = jnp.float32
ORTHO = 1.0 / math.sqrt(NX * NY * NZ)


def host_tables(length, modes_count, signed):
    frequency = np.arange(modes_count)
    if signed:
        frequency = np.concatenate([frequency, frequency - modes_count])
    phase = np.mod(np.arange(length)[:, None] * frequency[None, :], length)
    angles = phase.astype(np.float32) * np.float32(2.0 * math.pi / length)
    cos = np.cos(angles).astype(jnp.bfloat16).astype(np.float32)
    sin = np.sin(angles).astype(jnp.bfloat16).astype(np.float32)
    return cos, sin


def fixed_operands():
    cz, sz = host_tables(NZ, M, False)
    cy, sy = host_tables(NY, M, True)
    cx, sx = host_tables(NX, M, True)
    z_ops = np.zeros((8, NZ, 2, 8, M), np.float32)
    for c in range(8):
        z_ops[c, :, 0, c] = cz
        z_ops[c, :, 1, c] = -sz
    z_ops = z_ops.reshape(8 * NZ, 16 * M)
    y_all = np.stack([np.concatenate([cy.T, sy.T], 1), np.concatenate([-sy.T, cy.T], 1)], 1)
    y_all = y_all.reshape(8, 4, 2, 2 * NY)
    x_all = np.stack([np.stack([cx.T, sx.T], 1), np.stack([-sx.T, cx.T], 1)], 0)
    x_all = x_all.reshape(2, M, 2, 2, 8, 16).transpose(2, 0, 1, 3, 4, 5)
    order = [[[s ^ (4 * j + k) for j in range(2)] for k in range(4)] for s in range(8)]
    y_ops = np.stack([y_all[order[s]] for s in range(8)]).reshape(8, 64, 2 * NY)
    x_ops = np.stack([x_all[..., [s ^ k for k in range(4)], :] for s in range(8)])
    x_ops = x_ops.reshape(8, 64, NX)
    shuffle = np.zeros((4, 8, M, 8, 2, 4, M), np.float32)
    for b in range(4):
        for c in range(8):
            for d in range(M):
                shuffle[b, c, d, c, :, b, d] = 1.0
    shuffle = shuffle.reshape(32 * M, 64 * M)
    ops = dict(z_fwd=z_ops, z_back=z_ops.T, y=y_ops, x=x_ops, spread=shuffle)
    return {k: jnp.asarray(np.ascontiguousarray(v).astype(jnp.bfloat16)) for k, v in ops.items()}


def dot(a, b):
    return jnp.dot(a, b, preferred_element_type=F32)


def params(mib):
    return pltpu.CompilerParams(vmem_limit_bytes=mib << 20)


def cost(us, mib=1):
    return pl.CostEstimate(
        flops=int(us * 6e6), bytes_accessed=mib << 10, transcendentals=0
    )


VMEM = pl.BlockSpec(memory_space=pltpu.VMEM)
SMEM = pl.BlockSpec(memory_space=pltpu.SMEM)
HBM = pl.BlockSpec(memory_space=pltpu.HBM)
UNREAD = pl.BlockSpec(memory_space=pl.ANY)


def in_vmem(x):
    return pltpu.with_memory_space_constraint(x, pltpu.VMEM)


def in_hbm(x):
    return pltpu.with_memory_space_constraint(x, pltpu.HBM)


GROUP = 4
SLOTS = 12


def lateral_kernel(me_ref, v_ref, z_hbm, y_hbm, _, *rest):
    outs, (s_ref, z_ref, y_ref, b_ref, sem, z_sem) = rest[:4], rest[4:]
    nx = v_ref.shape[0]

    def copy(x):
        slot = lax.rem(x, SLOTS)
        return pltpu.make_async_copy(v_ref.at[x], b_ref.at[slot], sem.at[slot])

    tables = [
        pltpu.make_async_copy(z_hbm, z_ref, z_sem.at[0]),
        pltpu.make_async_copy(y_hbm.at[me_ref[0]], y_ref, z_sem.at[1]),
    ]
    for x in range(GROUP):
        copy(x).start()
    for table in tables:
        table.start()
    for x in range(GROUP, SLOTS - GROUP):
        copy(x).start()
    for table in tables:
        table.wait()

    def one(i, carry):
        for k in range(GROUP):
            x = i * GROUP + k
            ahead = x + SLOTS - GROUP

            @pl.when(ahead < nx)
            def _():
                copy(ahead).start()

            copy(x).wait()
        rows = [
            jnp.concatenate(
                [b_ref[lax.rem(i * GROUP + k, SLOTS), co * 8 + c] for c in range(8)], axis=1
            )
            for k in range(GROUP)
            for co in range(4)
        ]
        along = dot(jnp.concatenate(rows, axis=0), z_ref[...]).astype(BF)
        for k in range(GROUP):
            for h in range(2):
                at = (k * 2 + h) * 256
                lo = along[at : at + 128]
                hi = along[at + 128 : at + 256]
                rhs = jnp.concatenate(
                    [
                        jnp.concatenate([lo[:, :128], hi[:, :128]], axis=1),
                        jnp.concatenate([lo[:, 128:], hi[:, 128:]], axis=1),
                    ],
                    axis=0,
                )
                out = dot(y_ref[...], rhs)
                for j in range(2):
                    s_ref[h * 2 + j, pl.ds(i * GROUP + k, 64, stride=16), :] = out[
                        :, j * 128 : j * 128 + 128
                    ]
        return carry

    lax.fori_loop(0, nx // GROUP, one, 0)
    for r in range(64):
        q, j, k = r // 16, (r // 8) % 2, r % 8
        for n in range(4):
            cut = s_ref[n, r * 16 : r * 16 + 16, :].astype(BF)
            outs[q][j, :, k * 512 + n * 128 : k * 512 + n * 128 + 128] = cut


def lateral(me, values, ops, first, name):
    nx = values.shape[0]
    return pl.pallas_call(
        lateral_kernel,
        in_specs=[SMEM, HBM, HBM, HBM, UNREAD],
        out_specs=[VMEM] * 4,
        out_shape=[jax.ShapeDtypeStruct((2, nx, 4096), BF)] * 4,
        scratch_shapes=[
            pltpu.VMEM((4, nx * 64, 128), F32),
            pltpu.VMEM((1024, 256), BF),
            pltpu.VMEM((64, 256), BF),
            pltpu.VMEM((SLOTS, 32, NY, NZ), BF),
            pltpu.SemaphoreType.DMA((SLOTS,)),
            pltpu.SemaphoreType.DMA((2,)),
        ],
        compiler_params=params(20),
        cost_estimate=cost(10),
        name=name,
    )(me, in_hbm(values), in_hbm(ops["z_fwd"]), in_hbm(ops["y"]), first)


def square_sum(table, refs, j, b):
    rhs = jnp.concatenate(
        [ref[j, :, pl.ds(b * 1024 + part * 512, 512)] for part in range(2) for ref in refs],
        axis=0,
    )
    return dot(table, rhs)


def partner_kernel(me_ref, r0, r1, r2, r3, x_hbm, _, o_ref, __, x_ref, sem):
    copy = pltpu.make_async_copy(x_hbm.at[me_ref[0]], x_ref, sem)
    copy.start()
    copy.wait()
    for b in range(4):
        o_ref[:, pl.ds(b * 512, 512)] = square_sum(x_ref[...], (r0, r1, r2, r3), 1, b).astype(BF)


def partner_modes(me, received, ops, passed, name):
    return pl.pallas_call(
        partner_kernel,
        in_specs=[SMEM] + [VMEM] * 4 + [HBM, UNREAD],
        out_specs=[VMEM, UNREAD],
        out_shape=[
            jax.ShapeDtypeStruct((64, 2048), BF),
            jax.ShapeDtypeStruct(passed.shape, passed.dtype),
        ],
        input_output_aliases={6: 1},
        scratch_shapes=[pltpu.VMEM((64, NX), BF), pltpu.SemaphoreType.DMA(())],
        compiler_params=params(16),
        cost_estimate=cost(1),
        name=name,
    )(me, *received, in_hbm(ops["x"]), passed)


def axial_modes(table, refs, other_ref, spread_ref, ready, doubled, store):
    lane = lax.broadcasted_iota(jnp.int32, (1, 512), 1)
    scale = jnp.where(lane % M == 0, ORTHO, (2.0 if doubled else 1.0) * ORTHO).astype(F32)
    cuts = [
        (
            (square_sum(table, refs, 0, b) + other_ref[:, pl.ds(b * 512, 512)].astype(F32)) * scale
        ).astype(BF)
        for b in range(4)
    ]
    both = jnp.concatenate(
        [
            jnp.concatenate(
                [cut[a2 * 32 : a2 * 32 + 32, co * 128 : co * 128 + 128] for cut in cuts], axis=1
            )
            for a2 in range(2)
            for co in range(4)
        ],
        axis=0,
    )
    low = lax.broadcasted_iota(jnp.int32, (128, 128), 1) < 64
    ready()
    for c in range(0, 8, 2):
        moved = dot(both, spread_ref[:, pl.ds(c * 128, 256)])
        for k in range(2):
            cut = moved[:, k * 128 : k * 128 + 128]
            store(c + k, jnp.where(low, cut[:128], cut[128:]))


def volume_modes_kernel(
    me_ref, r0, r1, r2, r3, other_ref, x_hbm, spread_hbm, *rest
):
    o_ref, x_ref, spread_ref, sem = rest[-4:]
    copies = [
        pltpu.make_async_copy(x_hbm.at[me_ref[0]], x_ref, sem.at[0]),
        pltpu.make_async_copy(spread_hbm, spread_ref, sem.at[1]),
    ]
    for copy in copies:
        copy.start()

    def store(c, value):
        for co in range(4):
            o_ref[co * 8 + c] = value[co * 32 : co * 32 + 32].astype(BF)

    copies[0].wait()
    axial_modes(
        x_ref[...], (r0, r1, r2, r3), other_ref, spread_ref, copies[1].wait, False, store
    )


MODE_SCRATCH = [
    pltpu.VMEM((64, NX), BF),
    pltpu.VMEM((512, 1024), BF),
    pltpu.SemaphoreType.DMA((2,)),
]


def volume_modes(me, received, other, ops, ahead):
    return pl.pallas_call(
        volume_modes_kernel,
        in_specs=[SMEM] + [VMEM] * 5 + [HBM] * 2 + [HBM] * len(ahead),
        out_specs=VMEM,
        out_shape=jax.ShapeDtypeStruct((32, 32, 128), BF),
        scratch_shapes=MODE_SCRATCH,
        compiler_params=params(16),
        cost_estimate=cost(1.5),
        name="volume_modes",
    )(me, *received, other, in_hbm(ops["x"]), in_hbm(ops["spread"]), *ahead)


def kron_operand(at, p_ref, gain_ref):
    lane = lax.broadcasted_iota(jnp.int32, (32, 128), 1)
    here = lane == lax.rem(at, 128)
    gain = jnp.sum(jnp.where(here, gain_ref[...].astype(F32), 0.0), axis=1, keepdims=True)
    wide = (
        lax.broadcasted_iota(jnp.int32, (32, 256), 0)
        == lax.broadcasted_iota(jnp.int32, (32, 256), 1) // 8
    )
    tall = (
        lax.broadcasted_iota(jnp.int32, (256, 32), 0) // 8
        == lax.broadcasted_iota(jnp.int32, (256, 32), 1)
    )
    gains = jnp.sum(jnp.where(wide, gain, 0.0), axis=0, keepdims=True)
    kron = dot(tall.astype(F32).astype(BF), p_ref[...]).astype(BF)
    kron = dot(kron, wide.astype(F32).astype(BF)) * gains
    same = lax.rem(lax.broadcasted_iota(jnp.int32, (256, 256), 0), 8) == lax.rem(
        lax.broadcasted_iota(jnp.int32, (256, 256), 1), 8
    )
    return jnp.where(same, kron, 0.0).astype(BF)


def pack_kernel(
    at_ref, w_hbm, p_ref, g_hbm, _, o_ref, k_ref, w_ref, gain_ref, sem, gain_sem
):
    block = pl.multiple_of(at_ref[0] // 128 * 128, 128)
    gains = pltpu.make_async_copy(g_hbm.at[:, pl.ds(block, 128)], gain_ref, gain_sem)
    gains.start()
    slots = w_ref.shape[0]

    def copy(i):
        slot = lax.rem(i, slots)
        return pltpu.make_async_copy(w_hbm.at[:, pl.ds(2 * i, 2)], w_ref.at[slot], sem.at[slot])

    for i in range(slots - 1):
        copy(i).start()

    gains.wait()
    k_ref[...] = kron_operand(at_ref[0], p_ref, gain_ref)

    def one(i, carry):
        @pl.when(i + slots - 1 < M)
        def _():
            copy(i + slots - 1).start()

        copy(i).wait()
        slot = lax.rem(i, slots)
        for part in range(2):
            o_ref[part, i] = jnp.concatenate(
                [w_ref[slot, part, 0], w_ref[slot, part, 1]], axis=-1
            )
        return carry

    lax.fori_loop(0, M, one, 0)


def pack_weight(bias_index, weight, pointwise_weight, gain_table, first):
    return pl.pallas_call(
        pack_kernel,
        in_specs=[SMEM, HBM, VMEM, HBM, UNREAD],
        out_specs=[VMEM, VMEM],
        out_shape=[
            pltpu.VMEM((2, M, 32, 32, 128), BF),
            pltpu.HBM((256, 256), BF),
        ],
        scratch_shapes=[
            pltpu.VMEM((9, 2, 2, 32, 32, 64), BF),
            pltpu.VMEM((32, 128), BF),
            pltpu.SemaphoreType.DMA((9,)),
            pltpu.SemaphoreType.DMA(()),
        ],
        compiler_params=params(16),
        cost_estimate=cost(8),
        name="pack_weight",
    )(bias_index, in_hbm(weight), pointwise_weight, in_hbm(gain_table.T), first)


def back_modes_kernel(
    me_ref, r0, r1, r2, r3, other_ref, x_hbm, w_ref, spread_hbm, g_ref, o_ref,
    x_ref, spread_ref, sem, g_s, b_s, t_s,
):
    copies = [
        pltpu.make_async_copy(x_hbm.at[me_ref[0]], x_ref, sem.at[0]),
        pltpu.make_async_copy(spread_hbm, spread_ref, sem.at[1]),
    ]
    for copy in copies:
        copy.start()

    def store(c, value):
        for co in range(4):
            cut = value[co * 32 : co * 32 + 32]
            g_ref[co * 8 + c] = cut.astype(BF)
            g_s[pl.ds((co * 8 + c) * 32, 32), :] = cut

    copies[0].wait()
    axial_modes(
        x_ref[...], (r0, r1, r2, r3), other_ref, spread_ref, copies[1].wait, True, store
    )

    def line(i, carry):
        g_re = g_s[pl.ds(i, 32, stride=32), :]
        g_im = g_s[pl.ds(i + 16, 32, stride=32), :]
        for c in range(32):
            w_re = w_ref[0, i, c].astype(F32)
            w_im = w_ref[1, i, c].astype(F32)
            re = w_re * g_re + w_im * g_im
            im = w_re * g_im - w_im * g_re
            t_s[0, c * 8 : c * 8 + 8, :] = (re[:8] + re[8:16]) + (re[16:24] + re[24:])
            t_s[1, c * 8 : c * 8 + 8, :] = (im[:8] + im[8:16]) + (im[16:24] + im[24:])
        for part in range(2):
            total = t_s[part, pl.ds(0, 32, stride=8), :]
            for k in range(1, 8):
                total = total + t_s[part, pl.ds(k, 32, stride=8), :]
            b_s[pl.ds(pl.multiple_of((part * 16 + i) * 32, 32), 32), :] = total * ORTHO
        return carry

    lax.fori_loop(0, M, line, 0)
    low = lax.broadcasted_iota(jnp.int32, (32, 128), 1) < 64
    stacks = [[], []]
    for co in range(4):
        cuts = [b_s[pl.ds(co * 8 + c, 32, stride=32), :] for c in range(8)]
        for a2 in range(2):
            keep = low if a2 == 0 else jnp.logical_not(low)
            stacks[a2].append(
                jnp.concatenate([jnp.where(keep, cut, 0.0).astype(BF) for cut in cuts], axis=1)
            )
    moved = lax.dot_general(
        jnp.concatenate(stacks[0] + stacks[1], axis=0),
        spread_ref[...],
        (((1,), (1,)), ((), ())),
        preferred_element_type=F32,
    ).astype(BF)
    for a2 in range(2):
        for co in range(4):
            at = (a2 * 4 + co) * 32
            o_ref[a2 * 32 : a2 * 32 + 32, co * 512 : co * 512 + 512] = moved[at : at + 32]


def back_modes(me, received, other, packed, ops):
    return pl.pallas_call(
        back_modes_kernel,
        in_specs=[SMEM] + [VMEM] * 5 + [HBM, VMEM, HBM],
        out_specs=[VMEM, VMEM],
        out_shape=[
            jax.ShapeDtypeStruct((32, 32, 128), BF),
            jax.ShapeDtypeStruct((64, 2048), BF),
        ],
        scratch_shapes=MODE_SCRATCH
        + [
            pltpu.VMEM((1024, 128), F32),
            pltpu.VMEM((1024, 128), F32),
            pltpu.VMEM((2, 256, 128), F32),
        ],
        compiler_params=params(10),
        cost_estimate=cost(6),
        name="back_modes",
    )(me, *received, other, in_hbm(ops["x"]), in_vmem(packed), in_hbm(ops["spread"]))


def planes_kernel(me_ref, b_ref, x_hbm, *rest):
    outs, (x_ref, sem) = rest[-6:-2], rest[-2:]
    copy = pltpu.make_async_copy(x_hbm.at[me_ref[0]], x_ref, sem)
    copy.start()
    copy.wait()
    table = x_ref[...].astype(F32).T.astype(BF)
    for co in range(4):
        planes = dot(table, b_ref[:, pl.ds(co * 512, 512)]).astype(BF)
        for part in range(2):
            for b in range(4):
                lane = (b * 2 + part) * 512 + co * 128
                for q in range(4):
                    outs[q][:, lane : lane + 128] = planes[
                        part * 64 + q * 16 : part * 64 + q * 16 + 16, b * 128 : b * 128 + 128
                    ]


def back_planes(me, modes, ops, first, name, ahead=(), far=()):
    return pl.pallas_call(
        planes_kernel,
        in_specs=[SMEM, VMEM, HBM, UNREAD] + [UNREAD] * len(ahead) + [HBM] * len(far),
        out_specs=[UNREAD] + [VMEM] * 4,
        out_shape=[jax.ShapeDtypeStruct(first.shape, first.dtype)]
        + [jax.ShapeDtypeStruct((16, 4096), BF)] * 4,
        input_output_aliases={3: 0},
        scratch_shapes=[pltpu.VMEM((64, NX), BF), pltpu.SemaphoreType.DMA(())],
        compiler_params=params(16),
        cost_estimate=cost(1),
        name=name,
    )(me, modes, in_hbm(ops["x"]), first, *ahead, *[in_hbm(x) for x in far])


def weight_grad_kernel(half_ref, u0_ref, u1_ref, g0_ref, g1_ref, o_ref, u_s, g_s):
    i = pl.program_id(0)
    lines = o_ref.shape[1] // 2

    @pl.when(i == 0)
    def _():
        for s, (u, g) in enumerate(((u0_ref, g0_ref), (u1_ref, g1_ref))):
            u_s[s] = u[...].reshape(1024, 128).astype(F32)
            g_s[s] = g[...].reshape(1024, 128).astype(F32)

    base = half_ref[0] * 512
    for k in range(lines):
        at = i * lines + k
        u = [[u_s[s, pl.ds(at + 16 * r, 32, stride=32), :] for r in range(2)] for s in range(2)]
        g = [
            [g_s[s, pl.ds(base + at + 16 * r, 16, stride=32), :] for r in range(2)]
            for s in range(2)
        ]
        for c in range(32):
            row = [
                [jnp.broadcast_to(u[s][r][c : c + 1], (16, 128)) for r in range(2)]
                for s in range(2)
            ]
            re = (row[0][0] * g[0][0] + row[0][1] * g[0][1]) + (
                row[1][0] * g[1][0] + row[1][1] * g[1][1]
            )
            im = (row[0][0] * g[0][1] - row[0][1] * g[0][0]) + (
                row[1][0] * g[1][1] - row[1][1] * g[1][0]
            )
            o_ref[0, 2 * k, c] = re[:, :64]
            o_ref[0, 2 * k + 1, c] = re[:, 64:]
            o_ref[1, 2 * k, c] = im[:, :64]
            o_ref[1, 2 * k + 1, c] = im[:, 64:]


def weight_grad(half, u0, u1, g0, g1):
    return pl.pallas_call(
        weight_grad_kernel,
        grid=(4,),
        in_specs=[SMEM] + [VMEM] * 4,
        out_specs=pl.BlockSpec((2, 8, 32, 16, 64), lambda i: (0, i, 0, 0, 0)),
        scratch_shapes=[pltpu.VMEM((2, 1024, 128), F32), pltpu.VMEM((2, 1024, 128), F32)],
        out_shape=jax.ShapeDtypeStruct((2, 32, 32, 16, 64), F32),
        compiler_params=params(16),
        cost_estimate=cost(8),
        name="weight_grad",
    )(half, u0, u1, g0, g1)


def pointwise_kernel(base, v_ref, k_hbm, _, o_ref, __, k_ref, i_ref, in_sem, k_sem):
    nx = o_ref.shape[0]
    slots = i_ref.shape[0]

    def load(x):
        slot = lax.rem(x, slots)
        return pltpu.make_async_copy(v_ref.at[base + x], i_ref.at[slot], in_sem.at[slot])

    table = pltpu.make_async_copy(k_hbm, k_ref, k_sem)
    table.start()
    for x in range(slots - 1):
        load(x).start()
    table.wait()

    def one(x, carry):
        @pl.when(x + slots - 1 < nx)
        def _():
            load(x + slots - 1).start()

        load(x).wait()
        slot = lax.rem(x, slots)
        for y in range(8):
            cut = i_ref[slot, :, y * 16 : y * 16 + 16, :].astype(F32)
            rhs = jnp.concatenate(
                [
                    cut[:, :8].reshape(256, 128).astype(BF),
                    cut[:, 8:].reshape(256, 128).astype(BF),
                ],
                axis=1,
            )
            point = dot(k_ref[...], rhs)
            o_ref[x, :, y * 16 : y * 16 + 16, :] = jnp.concatenate(
                [point[:, :128].reshape(32, 8, 128), point[:, 128:].reshape(32, 8, 128)], axis=1
            ).astype(BF)
        return carry

    lax.fori_loop(0, nx, one, 0)


def pointwise_save_kernel(base, v_ref, k_hbm, _, o_hbm, __, b_ref, out_sem, *scratch):
    k_ref, i_ref, in_sem, k_sem = scratch
    nx = o_hbm.shape[0]
    slots = i_ref.shape[0]

    def load(x):
        slot = lax.rem(x, slots)
        return pltpu.make_async_copy(v_ref.at[base + x], i_ref.at[slot], in_sem.at[slot])

    def save(x):
        slot = lax.rem(x, slots)
        return pltpu.make_async_copy(b_ref.at[slot], o_hbm.at[x], out_sem.at[slot])

    table = pltpu.make_async_copy(k_hbm, k_ref, k_sem)
    table.start()
    for x in range(slots - 1):
        load(x).start()
    table.wait()

    def one(x, carry):
        @pl.when(x + slots - 1 < nx)
        def _():
            load(x + slots - 1).start()

        @pl.when(x >= slots)
        def _():
            save(x - slots).wait()

        load(x).wait()
        slot = lax.rem(x, slots)
        for y in range(8):
            cut = i_ref[slot, :, y * 16 : y * 16 + 16, :].astype(F32)
            rhs = jnp.concatenate(
                [
                    cut[:, :8].reshape(256, 128).astype(BF),
                    cut[:, 8:].reshape(256, 128).astype(BF),
                ],
                axis=1,
            )
            point = dot(k_ref[...], rhs)
            b_ref[slot, :, y * 16 : y * 16 + 16, :] = jnp.concatenate(
                [point[:, :128].reshape(32, 8, 128), point[:, 128:].reshape(32, 8, 128)], axis=1
            ).astype(BF)
        save(x).start()
        return carry

    lax.fori_loop(0, nx, one, 0)
    for x in range(nx - slots, nx):
        save(x).wait()


def pointwise(cotangent, kron, base, count, first, keep, name):
    shape = (count, 32, NY, NZ)
    scratch = [
        pltpu.VMEM((256, 256), BF),
        pltpu.VMEM((4, 32, NY, NZ), BF),
        pltpu.SemaphoreType.DMA((4,)),
        pltpu.SemaphoreType.DMA(()),
    ]
    if not keep:
        scratch = [pltpu.VMEM((4, 32, NY, NZ), BF), pltpu.SemaphoreType.DMA((4,))] + scratch
    return pl.pallas_call(
        functools.partial(pointwise_kernel if keep else pointwise_save_kernel, base),
        in_specs=[HBM, HBM, UNREAD],
        out_specs=[VMEM if keep else HBM, UNREAD],
        out_shape=[
            pltpu.VMEM(shape, BF) if keep else pltpu.HBM(shape, BF),
            jax.ShapeDtypeStruct(first.shape, first.dtype),
        ],
        input_output_aliases={2: 1},
        scratch_shapes=scratch,
        compiler_params=params(12),
        cost_estimate=cost(5),
        name=name,
    )(in_hbm(cotangent), in_hbm(kron), first)


def finish_kernel(
    me_ref, n0, n1, n2, n3, f0, f1, f2, f3, p_ref, q_ref, y_hbm, z_hbm, o_ref,
    s_ref, i_ref, b_ref, yt_ref, y_ref, z_ref, in_sem, out_sem, sem,
):
    received = ((n0, n1, n2, n3), (f0, f1, f2, f3))
    split = p_ref.shape[0]
    total = o_ref.shape[0]
    slots = b_ref.shape[0]

    def load(x):
        slot = lax.rem(x, i_ref.shape[0])
        return pltpu.make_async_copy(p_ref.at[x], i_ref.at[slot], in_sem.at[slot])

    def place(t):
        return lax.rem(t + split, total)

    def save(t):
        slot = lax.rem(t, slots)
        return pltpu.make_async_copy(b_ref.at[slot], o_ref.at[place(t)], out_sem.at[slot])

    tables = [
        pltpu.make_async_copy(y_hbm.at[me_ref[0]], yt_ref, sem.at[0]),
        pltpu.make_async_copy(z_hbm, z_ref, sem.at[1]),
    ]
    for table in tables:
        table.start()
    for r in range(64):
        q, j, k = r // 16, (r // 8) % 2, r % 8
        for n in range(4):
            s_ref[n, r * 16 : r * 16 + 16, :] = received[j][q][
                :, k * 512 + n * 128 : k * 512 + n * 128 + 128
            ].astype(F32)
    for table in tables:
        table.wait()
    y_ref[...] = yt_ref[...].astype(F32).T.astype(BF)
    for x in range(i_ref.shape[0]):
        load(x).start()

    def pair(t, points):
        for k in range(2):

            @pl.when(t + k >= slots)
            def _():
                save(t + k - slots).wait()

        sides = []
        for k in range(2):
            x = place(t + k)
            planes = jnp.concatenate(
                [s_ref[n, pl.ds(x, 64, stride=16), :].astype(BF) for n in range(4)], axis=1
            )
            rows = dot(y_ref[...], planes).astype(BF)
            sides += [
                jnp.concatenate(
                    [rows[:128, co * 128 : co * 128 + 128], rows[128:, co * 128 : co * 128 + 128]],
                    axis=1,
                )
                for co in range(4)
            ]
        lhs = jnp.concatenate(sides, axis=0)
        for n in range(4):
            part = dot(lhs, z_ref[:, n * 256 : n * 256 + 256])
            for k in range(2):
                slot = lax.rem(t + k, slots)
                for co in range(4):
                    for j in range(2):
                        c = co * 8 + n * 2 + j
                        row = (k * 4 + co) * 128
                        b_ref[slot, c] = (
                            part[row : row + 128, j * 128 : j * 128 + 128]
                            + points[k][c].astype(F32)
                        ).astype(BF)
        for k in range(2):
            save(t + k).start()

    def kept(i, carry):
        pair(2 * i, [q_ref.at[2 * i + k] for k in range(2)])
        return carry

    def loaded(i, carry):
        ring = i_ref.shape[0]
        for k in range(2):
            load(2 * i + k).wait()
        pair(2 * i + total - split, [i_ref.at[lax.rem(2 * i + k, ring)] for k in range(2)])
        for k in range(2):

            @pl.when(2 * i + k + ring < split)
            def _():
                load(2 * i + k + ring).start()

        return carry

    lax.fori_loop(0, (total - split) // 2, kept, 0)
    lax.fori_loop(0, split // 2, loaded, 0)
    for t in range(total - slots, total):
        save(t).wait()


def finish(me, near, far, saved, kept, ops):
    nx = saved.shape[0] + kept.shape[0]
    shape = (nx,) + saved.shape[1:]
    return pl.pallas_call(
        finish_kernel,
        in_specs=[SMEM] + [VMEM] * 8 + [HBM, VMEM, HBM, HBM],
        out_specs=HBM,
        out_shape=jax.ShapeDtypeStruct(shape, BF),
        scratch_shapes=[
            pltpu.VMEM((4, nx * 64, 128), F32),
            pltpu.VMEM((4, 32, NY, NZ), BF),
            pltpu.VMEM((4, 32, NY, NZ), BF),
            pltpu.VMEM((64, 256), BF),
            pltpu.VMEM((256, 64), BF),
            pltpu.VMEM((256, 1024), BF),
            pltpu.SemaphoreType.DMA((4,)),
            pltpu.SemaphoreType.DMA((4,)),
            pltpu.SemaphoreType.DMA((2,)),
        ],
        compiler_params=params(16),
        cost_estimate=cost(12),
        name="finish",
    )(
        me, *near, *far, in_hbm(saved), in_vmem(kept), in_hbm(ops["y"]), in_hbm(ops["z_back"])
    )


ACROSS = [(s, s ^ 4) for s in range(8)]
SWAP = [(0, 1), (1, 0)]


def in_square(blocks):
    return [blocks[0]] + [
        lax.ppermute(blocks[k], "space", [(s, s ^ k) for s in range(8)]) for k in (1, 2, 3)
    ]


def tuned_device(volume, cotangent, spectral_weight, pointwise_weight, gain_table, bias_index):
    ops = fixed_operands()
    nx = volume.shape[1]
    vol = volume.reshape(nx, 32, NY, NZ)
    cot = cotangent.reshape(nx, 32, NY, NZ)
    me = lax.axis_index("space").astype(jnp.int32).reshape(1)
    half = lax.axis_index("dp").astype(jnp.int32).reshape(1)
    weight = jnp.transpose(spectral_weight, (0, 1, 3, 4, 2))

    cot_blocks = lateral(me, cot, ops, me, "cotangent_lateral")
    cot_received = in_square(cot_blocks)
    vol_blocks = lateral(me, vol, ops, cot_blocks[0], "volume_lateral")
    cot_partner, passed = partner_modes(
        me, cot_received, ops, vol_blocks[1], "cotangent_partner"
    )
    other = lax.ppermute(cot_partner, "space", ACROSS)
    vol_received = in_square([vol_blocks[0], passed, vol_blocks[2], vol_blocks[3]])
    packed, kron = pack_weight(bias_index, weight, pointwise_weight, gain_table, cot_partner)
    g_modes, back_own = back_modes(me, cot_received, other, packed, ops)
    back_other = lax.ppermute(back_own, "space", ACROSS)
    vol_partner, _ = partner_modes(me, vol_received, ops, back_own, "volume_partner")
    vol_partner, *own_planes = back_planes(me, back_own, ops, vol_partner, "own_planes")
    back_near = in_square(own_planes)
    saved, back_near[0] = pointwise(
        cot, kron, 0, nx // 2, own_planes[0], False, "pointwise_first"
    )
    vol_partner, *other_planes = back_planes(
        me, back_other, ops, vol_partner, "partner_planes", back_near[1:], [saved]
    )
    back_far = in_square(other_planes)
    kept, back_far[0] = pointwise(
        cot, kron, nx // 2, nx - nx // 2, other_planes[0], True, "pointwise_second"
    )
    vol_other = lax.ppermute(vol_partner, "space", ACROSS)
    out = finish(me, back_near, back_far, saved, kept, ops)
    u_modes = volume_modes(me, vol_received, vol_other, ops, [in_hbm(out)])
    g_other = lax.ppermute(g_modes, "dp", SWAP)
    u_other = lax.ppermute(u_modes, "dp", SWAP)
    grad = weight_grad(half, u_modes, u_other, g_modes, g_other)
    return out.reshape(volume.shape), jnp.transpose(grad, (0, 1, 4, 2, 3))


def per_device(volume, cotangent, spectral_weight, pointwise_weight, gain_table, bias_index):
    fits = (
        volume.shape == (1, 16, 32, NY, NZ)
        and spectral_weight.shape == (2, 2 * M, 64, 32, 32)
        and lax.axis_size("space") == 8
        and lax.axis_size("dp") == 2
    )
    device = tuned_device if fits else general_device
    return device(
        volume, cotangent, spectral_weight, pointwise_weight, gain_table, bias_index
    )


def solution(mesh):
    return jax.shard_map(
        per_device,
        mesh=mesh,
        in_specs=(
            P(("parts", "dp"), "space", None, None, None),
            P(("parts", "dp"), "space", None, None, None),
            P(None, None, "space", None, None),
            P(),
            P(),
            P(("parts", "dp")),
        ),
        out_specs=(
            P(("parts", "dp"), "space", None, None, None),
            P("parts", None, "space", None, "dp"),
        ),
        check_vma=False,
    )
```

```python
import functools
import math

import jax
import jax.numpy as jnp
import numpy as np
from jax import lax
from jax.experimental import pallas as pl
from jax.experimental.pallas import tpu as pltpu
from jax.sharding import PartitionSpec as P

M = 16
NX = 128
NY = 128
NZ = 128


def trig_tables(length, modes_count, signed):
    positions = jnp.arange(length, dtype=jnp.int32)
    mode_base = jnp.arange(modes_count, dtype=jnp.int32)
    if signed:
        frequency = jnp.concatenate([mode_base, mode_base - modes_count])
    else:
        frequency = mode_base
    phase_index = jnp.mod(positions[:, None] * frequency[None, :], length)
    angles = phase_index.astype(jnp.float32) * (2.0 * math.pi / length)
    return (jnp.cos(angles).astype(jnp.bfloat16), jnp.sin(angles).astype(jnp.bfloat16))


def general_device(volume, cotangent, spectral_weight, pointwise_weight, gain_table, bias_index):
    cos_z, sin_z = trig_tables(NZ, M, False)
    cos_y, sin_y = trig_tables(NY, M, True)
    cos_x, sin_x = trig_tables(NX, M, True)
    table_z = jnp.concatenate([cos_z, -sin_z], axis=1)
    table_y = jnp.concatenate([cos_y, sin_y], axis=1)
    paired_y = jnp.stack([cos_y, sin_y], axis=1)
    table_x = jnp.concatenate([cos_x, sin_x], axis=1)
    paired_x = jnp.stack([cos_x, sin_x], axis=1)
    ortho_scale = 1.0 / math.sqrt(NX * NY * NZ)
    pair_count = spectral_weight.shape[2]
    global_pairs = lax.axis_index("space") * pair_count + jnp.arange(pair_count, dtype=jnp.int32)
    flat_scale = jnp.full((pair_count,), ortho_scale, dtype=jnp.float32)
    doubled_scale = jnp.where(global_pairs % M == 0, 1.0, 2.0).astype(jnp.float32) * ortho_scale

    def lateral_spectrum(values_in):
        along_z = jnp.einsum(
            "sxcyz,zk->sxcky", values_in, table_z, preferred_element_type=jnp.float32
        ).astype(jnp.bfloat16)
        products = jnp.einsum(
            "sxcky,yj->sxckj", along_z, table_y, preferred_element_type=jnp.float32
        )
        real_part = products[:, :, :, :M, : 2 * M] + products[:, :, :, M:, 2 * M :]
        imag_part = products[:, :, :, M:, : 2 * M] - products[:, :, :, :M, 2 * M :]
        stacked = jnp.swapaxes(jnp.stack([real_part, imag_part], axis=2), 4, 5).astype(jnp.bfloat16)
        return stacked.reshape(stacked.shape[0], stacked.shape[1], 2, stacked.shape[3], 2 * M * M)

    def axial_spectrum(received, pair_scale):
        products = jnp.einsum(
            "sxrcp,xj->srjpc", received, table_x, preferred_element_type=jnp.float32
        )
        real_part = products[:, 0, : 2 * M] + products[:, 1, 2 * M :]
        imag_part = products[:, 1, : 2 * M] - products[:, 0, 2 * M :]
        stacked = jnp.stack([real_part, imag_part], axis=1)
        return (stacked * pair_scale[None, None, None, :, None]).astype(jnp.bfloat16)

    volume_hat = axial_spectrum(
        lax.all_to_all(lateral_spectrum(volume), "space", split_axis=4, concat_axis=1, tiled=True),
        flat_scale,
    )
    cotangent_hat = axial_spectrum(
        lax.all_to_all(
            lateral_spectrum(cotangent), "space", split_axis=4, concat_axis=1, tiled=True
        ),
        doubled_scale,
    )
    grad_real = jnp.einsum(
        "sapc,sapo->apco", volume_hat[:, 0], cotangent_hat[:, 0], preferred_element_type=jnp.float32
    ) + jnp.einsum(
        "sapc,sapo->apco", volume_hat[:, 1], cotangent_hat[:, 1], preferred_element_type=jnp.float32
    )
    grad_imag = jnp.einsum(
        "sapc,sapo->apco", volume_hat[:, 0], cotangent_hat[:, 1], preferred_element_type=jnp.float32
    ) - jnp.einsum(
        "sapc,sapo->apco", volume_hat[:, 1], cotangent_hat[:, 0], preferred_element_type=jnp.float32
    )
    spectral_grad = lax.psum_scatter(
        jnp.stack([grad_real, grad_imag]).astype(jnp.bfloat16),
        "dp",
        scatter_dimension=4,
        tiled=True,
    ).astype(jnp.float32)
    weight_real = spectral_weight[0]
    weight_imag = spectral_weight[1]
    cot_real = cotangent_hat[:, 0]
    cot_imag = cotangent_hat[:, 1]
    back_real = jnp.einsum(
        "apco,sapo->sapc", weight_real, cot_real, preferred_element_type=jnp.float32
    ) + jnp.einsum("apco,sapo->sapc", weight_imag, cot_imag, preferred_element_type=jnp.float32)
    back_imag = jnp.einsum(
        "apco,sapo->sapc", weight_real, cot_imag, preferred_element_type=jnp.float32
    ) - jnp.einsum("apco,sapo->sapc", weight_imag, cot_real, preferred_element_type=jnp.float32)
    back_modes = jnp.stack([back_real, back_imag], axis=1).astype(jnp.bfloat16)
    products = jnp.einsum(
        "srapc,xta->srtxcp", back_modes, paired_x, preferred_element_type=jnp.float32
    )
    plane_real = products[:, 0, 0] - products[:, 1, 1]
    plane_imag = products[:, 0, 1] + products[:, 1, 0]
    back_planes = jnp.stack([plane_real, plane_imag], axis=2).astype(jnp.bfloat16)
    received = lax.all_to_all(back_planes, "space", split_axis=1, concat_axis=4, tiled=True)
    mode_grid = received.reshape(
        received.shape[0], received.shape[1], 2, received.shape[3], 2 * M, M
    )
    row_products = jnp.einsum(
        "nxrcbd,ytb->nxrtcyd", mode_grid, paired_y, preferred_element_type=jnp.float32
    )
    row_real = row_products[:, :, 0, 0] - row_products[:, :, 1, 1]
    row_imag = row_products[:, :, 0, 1] + row_products[:, :, 1, 0]
    row_values = jnp.concatenate([row_real, row_imag], axis=4).astype(jnp.bfloat16)
    spectral_part = (
        jnp.einsum("nxcyk,kz->nxcyz", row_values, table_z.T, preferred_element_type=jnp.float32)
        * ortho_scale
    )
    bias_rows = (
        bias_index[:, None] == jnp.arange(gain_table.shape[0], dtype=jnp.int32)[None, :]
    ).astype(jnp.bfloat16)
    gain_rows = jnp.dot(bias_rows, gain_table, preferred_element_type=jnp.float32)
    scaled = (cotangent * gain_rows[:, None, :, None, None]).astype(jnp.bfloat16)
    pointwise_part = jnp.einsum(
        "co,sxoyz->sxcyz", pointwise_weight, scaled, preferred_element_type=jnp.float32
    )
    return ((spectral_part + pointwise_part).astype(jnp.bfloat16), spectral_grad)


BF = jnp.bfloat16
F32 = jnp.float32
ORTHO = 1.0 / math.sqrt(NX * NY * NZ)


def host_tables(length, modes_count, signed):
    frequency = np.arange(modes_count)
    if signed:
        frequency = np.concatenate([frequency, frequency - modes_count])
    phase = np.mod(np.arange(length)[:, None] * frequency[None, :], length)
    angles = phase.astype(np.float32) * np.float32(2.0 * math.pi / length)
    cos = np.cos(angles).astype(jnp.bfloat16).astype(np.float32)
    sin = np.sin(angles).astype(jnp.bfloat16).astype(np.float32)
    return cos, sin


def fixed_operands():
    cz, sz = host_tables(NZ, M, False)
    cy, sy = host_tables(NY, M, True)
    cx, sx = host_tables(NX, M, True)
    z_ops = np.zeros((8, NZ, 2, 8, M), np.float32)
    for c in range(8):
        z_ops[c, :, 0, c] = cz
        z_ops[c, :, 1, c] = -sz
    z_ops = z_ops.reshape(8 * NZ, 16 * M)
    y_all = np.stack([np.concatenate([cy.T, sy.T], 1), np.concatenate([-sy.T, cy.T], 1)], 1)
    y_all = y_all.reshape(8, 4, 2, 2 * NY)
    x_all = np.stack([np.stack([cx.T, sx.T], 1), np.stack([-sx.T, cx.T], 1)], 0)
    x_all = x_all.reshape(2, M, 2, 2, 8, 16).transpose(2, 0, 1, 3, 4, 5)
    order = [[[s ^ (4 * j + k) for j in range(2)] for k in range(4)] for s in range(8)]
    y_ops = np.stack([y_all[order[s]] for s in range(8)]).reshape(8, 64, 2 * NY)
    x_ops = np.stack([x_all[..., [s ^ k for k in range(4)], :] for s in range(8)])
    x_ops = x_ops.reshape(8, 64, NX)
    shuffle = np.zeros((4, 8, M, 8, 2, 4, M), np.float32)
    for b in range(4):
        for c in range(8):
            for d in range(M):
                shuffle[b, c, d, c, :, b, d] = 1.0
    shuffle = shuffle.reshape(32 * M, 64 * M)
    ops = dict(z_fwd=z_ops, z_back=z_ops.T, y=y_ops, x=x_ops, spread=shuffle)
    return {k: jnp.asarray(np.ascontiguousarray(v).astype(jnp.bfloat16)) for k, v in ops.items()}


def dot(a, b):
    return jnp.dot(a, b, preferred_element_type=F32)


def params(mib):
    return pltpu.CompilerParams(vmem_limit_bytes=mib << 20)


def cost(us, mib=1):
    return pl.CostEstimate(
        flops=int(us * 6e6), bytes_accessed=mib << 10, transcendentals=0
    )


VMEM = pl.BlockSpec(memory_space=pltpu.VMEM)
SMEM = pl.BlockSpec(memory_space=pltpu.SMEM)
HBM = pl.BlockSpec(memory_space=pltpu.HBM)
UNREAD = pl.BlockSpec(memory_space=pl.ANY)


def in_vmem(x):
    return pltpu.with_memory_space_constraint(x, pltpu.VMEM)


def in_hbm(x):
    return pltpu.with_memory_space_constraint(x, pltpu.HBM)


GROUP = 4
SLOTS = 12


def lateral_kernel(me_ref, v_ref, z_hbm, y_hbm, _, *rest):
    outs, (s_ref, z_ref, y_ref, b_ref, sem, z_sem) = rest[:4], rest[4:]
    nx = v_ref.shape[0]

    def copy(x):
        slot = lax.rem(x, SLOTS)
        return pltpu.make_async_copy(v_ref.at[x], b_ref.at[slot], sem.at[slot])

    tables = [
        pltpu.make_async_copy(z_hbm, z_ref, z_sem.at[0]),
        pltpu.make_async_copy(y_hbm.at[me_ref[0]], y_ref, z_sem.at[1]),
    ]
    for x in range(GROUP):
        copy(x).start()
    for table in tables:
        table.start()
    for x in range(GROUP, SLOTS - GROUP):
        copy(x).start()
    for table in tables:
        table.wait()

    def one(i, carry):
        for k in range(GROUP):
            x = i * GROUP + k
            ahead = x + SLOTS - GROUP

            @pl.when(ahead < nx)
            def _():
                copy(ahead).start()

            copy(x).wait()
        rows = [
            jnp.concatenate(
                [b_ref[lax.rem(i * GROUP + k, SLOTS), co * 8 + c] for c in range(8)], axis=1
            )
            for k in range(GROUP)
            for co in range(4)
        ]
        along = dot(jnp.concatenate(rows, axis=0), z_ref[...]).astype(BF)
        for k in range(GROUP):
            for h in range(2):
                at = (k * 2 + h) * 256
                lo = along[at : at + 128]
                hi = along[at + 128 : at + 256]
                rhs = jnp.concatenate(
                    [
                        jnp.concatenate([lo[:, :128], hi[:, :128]], axis=1),
                        jnp.concatenate([lo[:, 128:], hi[:, 128:]], axis=1),
                    ],
                    axis=0,
                )
                out = dot(y_ref[...], rhs)
                for j in range(2):
                    s_ref[h * 2 + j, pl.ds(i * GROUP + k, 64, stride=16), :] = out[
                        :, j * 128 : j * 128 + 128
                    ]
        return carry

    lax.fori_loop(0, nx // GROUP, one, 0)
    for r in range(64):
        q, j, k = r // 16, (r // 8) % 2, r % 8
        for n in range(4):
            cut = s_ref[n, r * 16 : r * 16 + 16, :].astype(BF)
            outs[q][j, :, k * 512 + n * 128 : k * 512 + n * 128 + 128] = cut


def lateral(me, values, ops, first, name):
    nx = values.shape[0]
    return pl.pallas_call(
        lateral_kernel,
        in_specs=[SMEM, HBM, HBM, HBM, UNREAD],
        out_specs=[VMEM] * 4,
        out_shape=[jax.ShapeDtypeStruct((2, nx, 4096), BF)] * 4,
        scratch_shapes=[
            pltpu.VMEM((4, nx * 64, 128), F32),
            pltpu.VMEM((1024, 256), BF),
            pltpu.VMEM((64, 256), BF),
            pltpu.VMEM((SLOTS, 32, NY, NZ), BF),
            pltpu.SemaphoreType.DMA((SLOTS,)),
            pltpu.SemaphoreType.DMA((2,)),
        ],
        compiler_params=params(20),
        cost_estimate=cost(10),
        name=name,
    )(me, in_hbm(values), in_hbm(ops["z_fwd"]), in_hbm(ops["y"]), first)


def square_sum(table, refs, j, b):
    rhs = jnp.concatenate(
        [ref[j, :, pl.ds(b * 1024 + part * 512, 512)] for part in range(2) for ref in refs],
        axis=0,
    )
    return dot(table, rhs)


def partner_kernel(me_ref, r0, r1, r2, r3, x_hbm, _, o_ref, __, x_ref, sem):
    copy = pltpu.make_async_copy(x_hbm.at[me_ref[0]], x_ref, sem)
    copy.start()
    copy.wait()
    for b in range(4):
        o_ref[:, pl.ds(b * 512, 512)] = square_sum(x_ref[...], (r0, r1, r2, r3), 1, b).astype(BF)


def partner_modes(me, received, ops, passed, name):
    return pl.pallas_call(
        partner_kernel,
        in_specs=[SMEM] + [VMEM] * 4 + [HBM, UNREAD],
        out_specs=[VMEM, UNREAD],
        out_shape=[
            jax.ShapeDtypeStruct((64, 2048), BF),
            jax.ShapeDtypeStruct(passed.shape, passed.dtype),
        ],
        input_output_aliases={6: 1},
        scratch_shapes=[pltpu.VMEM((64, NX), BF), pltpu.SemaphoreType.DMA(())],
        compiler_params=params(16),
        cost_estimate=cost(1),
        name=name,
    )(me, *received, in_hbm(ops["x"]), passed)


def axial_modes(table, refs, other_ref, spread_ref, ready, doubled, store):
    lane = lax.broadcasted_iota(jnp.int32, (1, 512), 1)
    scale = jnp.where(lane % M == 0, ORTHO, (2.0 if doubled else 1.0) * ORTHO).astype(F32)
    cuts = [
        (
            (square_sum(table, refs, 0, b) + other_ref[:, pl.ds(b * 512, 512)].astype(F32)) * scale
        ).astype(BF)
        for b in range(4)
    ]
    both = jnp.concatenate(
        [
            jnp.concatenate(
                [cut[a2 * 32 : a2 * 32 + 32, co * 128 : co * 128 + 128] for cut in cuts], axis=1
            )
            for a2 in range(2)
            for co in range(4)
        ],
        axis=0,
    )
    low = lax.broadcasted_iota(jnp.int32, (128, 128), 1) < 64
    ready()
    for c in range(0, 8, 2):
        moved = dot(both, spread_ref[:, pl.ds(c * 128, 256)])
        for k in range(2):
            cut = moved[:, k * 128 : k * 128 + 128]
            store(c + k, jnp.where(low, cut[:128], cut[128:]))


def volume_modes_kernel(
    me_ref, r0, r1, r2, r3, other_ref, x_hbm, spread_hbm, *rest
):
    o_ref, x_ref, spread_ref, sem = rest[-4:]
    copies = [
        pltpu.make_async_copy(x_hbm.at[me_ref[0]], x_ref, sem.at[0]),
        pltpu.make_async_copy(spread_hbm, spread_ref, sem.at[1]),
    ]
    for copy in copies:
        copy.start()

    def store(c, value):
        for co in range(4):
            o_ref[co * 8 + c] = value[co * 32 : co * 32 + 32].astype(BF)

    copies[0].wait()
    axial_modes(
        x_ref[...], (r0, r1, r2, r3), other_ref, spread_ref, copies[1].wait, False, store
    )


MODE_SCRATCH = [
    pltpu.VMEM((64, NX), BF),
    pltpu.VMEM((512, 1024), BF),
    pltpu.SemaphoreType.DMA((2,)),
]


def volume_modes(me, received, other, ops, ahead):
    return pl.pallas_call(
        volume_modes_kernel,
        in_specs=[SMEM] + [VMEM] * 5 + [HBM] * 2 + [HBM] * len(ahead),
        out_specs=VMEM,
        out_shape=jax.ShapeDtypeStruct((32, 32, 128), BF),
        scratch_shapes=MODE_SCRATCH,
        compiler_params=params(16),
        cost_estimate=cost(1.5),
        name="volume_modes",
    )(me, *received, other, in_hbm(ops["x"]), in_hbm(ops["spread"]), *ahead)


def kron_operand(at, p_ref, gain_ref):
    lane = lax.broadcasted_iota(jnp.int32, (32, 128), 1)
    here = lane == lax.rem(at, 128)
    gain = jnp.sum(jnp.where(here, gain_ref[...].astype(F32), 0.0), axis=1, keepdims=True)
    wide = (
        lax.broadcasted_iota(jnp.int32, (32, 256), 0)
        == lax.broadcasted_iota(jnp.int32, (32, 256), 1) // 8
    )
    tall = (
        lax.broadcasted_iota(jnp.int32, (256, 32), 0) // 8
        == lax.broadcasted_iota(jnp.int32, (256, 32), 1)
    )
    gains = jnp.sum(jnp.where(wide, gain, 0.0), axis=0, keepdims=True)
    kron = dot(tall.astype(F32).astype(BF), p_ref[...]).astype(BF)
    kron = dot(kron, wide.astype(F32).astype(BF)) * gains
    same = lax.rem(lax.broadcasted_iota(jnp.int32, (256, 256), 0), 8) == lax.rem(
        lax.broadcasted_iota(jnp.int32, (256, 256), 1), 8
    )
    return jnp.where(same, kron, 0.0).astype(BF)


def pack_kernel(
    at_ref, w_hbm, p_ref, g_hbm, _, o_ref, k_ref, w_ref, gain_ref, sem, gain_sem
):
    block = pl.multiple_of(at_ref[0] // 128 * 128, 128)
    gains = pltpu.make_async_copy(g_hbm.at[:, pl.ds(block, 128)], gain_ref, gain_sem)
    gains.start()
    slots = w_ref.shape[0]

    def copy(i):
        slot = lax.rem(i, slots)
        return pltpu.make_async_copy(w_hbm.at[:, pl.ds(2 * i, 2)], w_ref.at[slot], sem.at[slot])

    for i in range(slots - 1):
        copy(i).start()

    gains.wait()
    k_ref[...] = kron_operand(at_ref[0], p_ref, gain_ref)

    def one(i, carry):
        @pl.when(i + slots - 1 < M)
        def _():
            copy(i + slots - 1).start()

        copy(i).wait()
        slot = lax.rem(i, slots)
        for part in range(2):
            o_ref[part, i] = jnp.concatenate(
                [w_ref[slot, part, 0], w_ref[slot, part, 1]], axis=-1
            )
        return carry

    lax.fori_loop(0, M, one, 0)


def pack_weight(bias_index, weight, pointwise_weight, gain_table, first):
    return pl.pallas_call(
        pack_kernel,
        in_specs=[SMEM, HBM, VMEM, HBM, UNREAD],
        out_specs=[VMEM, VMEM],
        out_shape=[
            pltpu.VMEM((2, M, 32, 32, 128), BF),
            pltpu.HBM((256, 256), BF),
        ],
        scratch_shapes=[
            pltpu.VMEM((9, 2, 2, 32, 32, 64), BF),
            pltpu.VMEM((32, 128), BF),
            pltpu.SemaphoreType.DMA((9,)),
            pltpu.SemaphoreType.DMA(()),
        ],
        compiler_params=params(16),
        cost_estimate=cost(8),
        name="pack_weight",
    )(bias_index, in_hbm(weight), pointwise_weight, in_hbm(gain_table.T), first)


def back_modes_kernel(
    me_ref, r0, r1, r2, r3, other_ref, x_hbm, w_ref, spread_hbm, g_ref, o_ref,
    x_ref, spread_ref, sem, g_s, b_s, t_s,
):
    copies = [
        pltpu.make_async_copy(x_hbm.at[me_ref[0]], x_ref, sem.at[0]),
        pltpu.make_async_copy(spread_hbm, spread_ref, sem.at[1]),
    ]
    for copy in copies:
        copy.start()

    def store(c, value):
        for co in range(4):
            cut = value[co * 32 : co * 32 + 32]
            g_ref[co * 8 + c] = cut.astype(BF)
            g_s[pl.ds((co * 8 + c) * 32, 32), :] = cut

    copies[0].wait()
    axial_modes(
        x_ref[...], (r0, r1, r2, r3), other_ref, spread_ref, copies[1].wait, True, store
    )

    def line(i, carry):
        g_re = g_s[pl.ds(i, 32, stride=32), :]
        g_im = g_s[pl.ds(i + 16, 32, stride=32), :]
        for c in range(32):
            w_re = w_ref[0, i, c].astype(F32)
            w_im = w_ref[1, i, c].astype(F32)
            re = w_re * g_re + w_im * g_im
            im = w_re * g_im - w_im * g_re
            t_s[0, c * 8 : c * 8 + 8, :] = (re[:8] + re[8:16]) + (re[16:24] + re[24:])
            t_s[1, c * 8 : c * 8 + 8, :] = (im[:8] + im[8:16]) + (im[16:24] + im[24:])
        for part in range(2):
            total = t_s[part, pl.ds(0, 32, stride=8), :]
            for k in range(1, 8):
                total = total + t_s[part, pl.ds(k, 32, stride=8), :]
            b_s[pl.ds(pl.multiple_of((part * 16 + i) * 32, 32), 32), :] = total * ORTHO
        return carry

    lax.fori_loop(0, M, line, 0)
    low = lax.broadcasted_iota(jnp.int32, (32, 128), 1) < 64
    stacks = [[], []]
    for co in range(4):
        cuts = [b_s[pl.ds(co * 8 + c, 32, stride=32), :] for c in range(8)]
        for a2 in range(2):
            keep = low if a2 == 0 else jnp.logical_not(low)
            stacks[a2].append(
                jnp.concatenate([jnp.where(keep, cut, 0.0).astype(BF) for cut in cuts], axis=1)
            )
    moved = lax.dot_general(
        jnp.concatenate(stacks[0] + stacks[1], axis=0),
        spread_ref[...],
        (((1,), (1,)), ((), ())),
        preferred_element_type=F32,
    ).astype(BF)
    for a2 in range(2):
        for co in range(4):
            at = (a2 * 4 + co) * 32
            o_ref[a2 * 32 : a2 * 32 + 32, co * 512 : co * 512 + 512] = moved[at : at + 32]


def back_modes(me, received, other, packed, ops):
    return pl.pallas_call(
        back_modes_kernel,
        in_specs=[SMEM] + [VMEM] * 5 + [HBM, VMEM, HBM],
        out_specs=[VMEM, VMEM],
        out_shape=[
            jax.ShapeDtypeStruct((32, 32, 128), BF),
            jax.ShapeDtypeStruct((64, 2048), BF),
        ],
        scratch_shapes=MODE_SCRATCH
        + [
            pltpu.VMEM((1024, 128), F32),
            pltpu.VMEM((1024, 128), F32),
            pltpu.VMEM((2, 256, 128), F32),
        ],
        compiler_params=params(10),
        cost_estimate=cost(6),
        name="back_modes",
    )(me, *received, other, in_hbm(ops["x"]), in_vmem(packed), in_hbm(ops["spread"]))


def planes_kernel(me_ref, b_ref, x_hbm, *rest):
    outs, (x_ref, sem) = rest[-6:-2], rest[-2:]
    copy = pltpu.make_async_copy(x_hbm.at[me_ref[0]], x_ref, sem)
    copy.start()
    copy.wait()
    table = x_ref[...].astype(F32).T.astype(BF)
    for co in range(4):
        planes = dot(table, b_ref[:, pl.ds(co * 512, 512)]).astype(BF)
        for part in range(2):
            for b in range(4):
                lane = (b * 2 + part) * 512 + co * 128
                for q in range(4):
                    outs[q][:, lane : lane + 128] = planes[
                        part * 64 + q * 16 : part * 64 + q * 16 + 16, b * 128 : b * 128 + 128
                    ]


def back_planes(me, modes, ops, first, name, ahead=(), far=()):
    return pl.pallas_call(
        planes_kernel,
        in_specs=[SMEM, VMEM, HBM, UNREAD] + [UNREAD] * len(ahead) + [HBM] * len(far),
        out_specs=[UNREAD] + [VMEM] * 4,
        out_shape=[jax.ShapeDtypeStruct(first.shape, first.dtype)]
        + [jax.ShapeDtypeStruct((16, 4096), BF)] * 4,
        input_output_aliases={3: 0},
        scratch_shapes=[pltpu.VMEM((64, NX), BF), pltpu.SemaphoreType.DMA(())],
        compiler_params=params(16),
        cost_estimate=cost(1),
        name=name,
    )(me, modes, in_hbm(ops["x"]), first, *ahead, *[in_hbm(x) for x in far])


def weight_grad_kernel(half_ref, u0_ref, u1_ref, g0_ref, g1_ref, o_ref, u_s, g_s):
    i = pl.program_id(0)
    lines = o_ref.shape[1] // 2

    @pl.when(i == 0)
    def _():
        for s, (u, g) in enumerate(((u0_ref, g0_ref), (u1_ref, g1_ref))):
            u_s[s] = u[...].reshape(1024, 128).astype(F32)
            g_s[s] = g[...].reshape(1024, 128).astype(F32)

    base = half_ref[0] * 512
    for k in range(lines):
        at = i * lines + k
        u = [[u_s[s, pl.ds(at + 16 * r, 32, stride=32), :] for r in range(2)] for s in range(2)]
        g = [
            [g_s[s, pl.ds(base + at + 16 * r, 16, stride=32), :] for r in range(2)]
            for s in range(2)
        ]
        for c in range(32):
            row = [
                [jnp.broadcast_to(u[s][r][c : c + 1], (16, 128)) for r in range(2)]
                for s in range(2)
            ]
            re = (row[0][0] * g[0][0] + row[0][1] * g[0][1]) + (
                row[1][0] * g[1][0] + row[1][1] * g[1][1]
            )
            im = (row[0][0] * g[0][1] - row[0][1] * g[0][0]) + (
                row[1][0] * g[1][1] - row[1][1] * g[1][0]
            )
            o_ref[0, 2 * k, c] = re[:, :64]
            o_ref[0, 2 * k + 1, c] = re[:, 64:]
            o_ref[1, 2 * k, c] = im[:, :64]
            o_ref[1, 2 * k + 1, c] = im[:, 64:]


def weight_grad(half, u0, u1, g0, g1):
    return pl.pallas_call(
        weight_grad_kernel,
        grid=(4,),
        in_specs=[SMEM] + [VMEM] * 4,
        out_specs=pl.BlockSpec((2, 8, 32, 16, 64), lambda i: (0, i, 0, 0, 0)),
        scratch_shapes=[pltpu.VMEM((2, 1024, 128), F32), pltpu.VMEM((2, 1024, 128), F32)],
        out_shape=jax.ShapeDtypeStruct((2, 32, 32, 16, 64), F32),
        compiler_params=params(16),
        cost_estimate=cost(8),
        name="weight_grad",
    )(half, u0, u1, g0, g1)


def pointwise_kernel(base, v_ref, k_hbm, _, o_ref, __, k_ref, i_ref, in_sem, k_sem):
    nx = o_ref.shape[0]
    slots = i_ref.shape[0]

    def load(x):
        slot = lax.rem(x, slots)
        return pltpu.make_async_copy(v_ref.at[base + x], i_ref.at[slot], in_sem.at[slot])

    table = pltpu.make_async_copy(k_hbm, k_ref, k_sem)
    table.start()
    for x in range(slots - 1):
        load(x).start()
    table.wait()

    def one(x, carry):
        @pl.when(x + slots - 1 < nx)
        def _():
            load(x + slots - 1).start()

        load(x).wait()
        slot = lax.rem(x, slots)
        for y in range(8):
            cut = i_ref[slot, :, y * 16 : y * 16 + 16, :].astype(F32)
            rhs = jnp.concatenate(
                [
                    cut[:, :8].reshape(256, 128).astype(BF),
                    cut[:, 8:].reshape(256, 128).astype(BF),
                ],
                axis=1,
            )
            point = dot(k_ref[...], rhs)
            o_ref[x, :, y * 16 : y * 16 + 16, :] = jnp.concatenate(
                [point[:, :128].reshape(32, 8, 128), point[:, 128:].reshape(32, 8, 128)], axis=1
            ).astype(BF)
        return carry

    lax.fori_loop(0, nx, one, 0)


def pointwise_save_kernel(base, v_ref, k_hbm, _, o_hbm, __, b_ref, out_sem, *scratch):
    k_ref, i_ref, in_sem, k_sem = scratch
    nx = o_hbm.shape[0]
    slots = i_ref.shape[0]

    def load(x):
        slot = lax.rem(x, slots)
        return pltpu.make_async_copy(v_ref.at[base + x], i_ref.at[slot], in_sem.at[slot])

    def save(x):
        slot = lax.rem(x, slots)
        return pltpu.make_async_copy(b_ref.at[slot], o_hbm.at[x], out_sem.at[slot])

    table = pltpu.make_async_copy(k_hbm, k_ref, k_sem)
    table.start()
    for x in range(slots - 1):
        load(x).start()
    table.wait()

    def one(x, carry):
        @pl.when(x + slots - 1 < nx)
        def _():
            load(x + slots - 1).start()

        @pl.when(x >= slots)
        def _():
            save(x - slots).wait()

        load(x).wait()
        slot = lax.rem(x, slots)
        for y in range(8):
            cut = i_ref[slot, :, y * 16 : y * 16 + 16, :].astype(F32)
            rhs = jnp.concatenate(
                [
                    cut[:, :8].reshape(256, 128).astype(BF),
                    cut[:, 8:].reshape(256, 128).astype(BF),
                ],
                axis=1,
            )
            point = dot(k_ref[...], rhs)
            b_ref[slot, :, y * 16 : y * 16 + 16, :] = jnp.concatenate(
                [point[:, :128].reshape(32, 8, 128), point[:, 128:].reshape(32, 8, 128)], axis=1
            ).astype(BF)
        save(x).start()
        return carry

    lax.fori_loop(0, nx, one, 0)
    for x in range(nx - slots, nx):
        save(x).wait()


def pointwise(cotangent, kron, base, count, first, keep, name):
    shape = (count, 32, NY, NZ)
    scratch = [
        pltpu.VMEM((256, 256), BF),
        pltpu.VMEM((4, 32, NY, NZ), BF),
        pltpu.SemaphoreType.DMA((4,)),
        pltpu.SemaphoreType.DMA(()),
    ]
    if not keep:
        scratch = [pltpu.VMEM((4, 32, NY, NZ), BF), pltpu.SemaphoreType.DMA((4,))] + scratch
    return pl.pallas_call(
        functools.partial(pointwise_kernel if keep else pointwise_save_kernel, base),
        in_specs=[HBM, HBM, UNREAD],
        out_specs=[VMEM if keep else HBM, UNREAD],
        out_shape=[
            pltpu.VMEM(shape, BF) if keep else pltpu.HBM(shape, BF),
            jax.ShapeDtypeStruct(first.shape, first.dtype),
        ],
        input_output_aliases={2: 1},
        scratch_shapes=scratch,
        compiler_params=params(12),
        cost_estimate=cost(5),
        name=name,
    )(in_hbm(cotangent), in_hbm(kron), first)


def finish_kernel(
    me_ref, n0, n1, n2, n3, f0, f1, f2, f3, p_ref, q_ref, y_hbm, z_hbm, o_ref,
    s_ref, i_ref, b_ref, yt_ref, y_ref, z_ref, in_sem, out_sem, sem,
):
    received = ((n0, n1, n2, n3), (f0, f1, f2, f3))
    split = p_ref.shape[0]
    total = o_ref.shape[0]
    slots = b_ref.shape[0]

    def load(x):
        slot = lax.rem(x, i_ref.shape[0])
        return pltpu.make_async_copy(p_ref.at[x], i_ref.at[slot], in_sem.at[slot])

    def place(t):
        return lax.rem(t + split, total)

    def save(t):
        slot = lax.rem(t, slots)
        return pltpu.make_async_copy(b_ref.at[slot], o_ref.at[place(t)], out_sem.at[slot])

    tables = [
        pltpu.make_async_copy(y_hbm.at[me_ref[0]], yt_ref, sem.at[0]),
        pltpu.make_async_copy(z_hbm, z_ref, sem.at[1]),
    ]
    for table in tables:
        table.start()
    for r in range(64):
        q, j, k = r // 16, (r // 8) % 2, r % 8
        for n in range(4):
            s_ref[n, r * 16 : r * 16 + 16, :] = received[j][q][
                :, k * 512 + n * 128 : k * 512 + n * 128 + 128
            ].astype(F32)
    for table in tables:
        table.wait()
    y_ref[...] = yt_ref[...].astype(F32).T.astype(BF)
    for x in range(i_ref.shape[0]):
        load(x).start()

    def step(t, point):
        @pl.when(t >= slots)
        def _():
            save(t - slots).wait()

        x = place(t)
        slot = lax.rem(t, slots)
        planes = jnp.concatenate(
            [s_ref[n, pl.ds(x, 64, stride=16), :].astype(BF) for n in range(4)], axis=1
        )
        rows = dot(y_ref[...], planes).astype(BF)
        lhs = jnp.concatenate(
            [
                jnp.concatenate(
                    [rows[:128, co * 128 : co * 128 + 128], rows[128:, co * 128 : co * 128 + 128]],
                    axis=1,
                )
                for co in range(4)
            ],
            axis=0,
        )
        for n in range(4):
            part = dot(lhs, z_ref[:, n * 256 : n * 256 + 256])
            for co in range(4):
                for j in range(2):
                    c = co * 8 + n * 2 + j
                    b_ref[slot, c] = (
                        part[co * 128 : co * 128 + 128, j * 128 : j * 128 + 128]
                        + point[c].astype(F32)
                    ).astype(BF)
        save(t).start()

    def kept(t, carry):
        step(t, q_ref.at[t])
        return carry

    def loaded(x, carry):
        load(x).wait()
        step(x + total - split, i_ref.at[lax.rem(x, i_ref.shape[0])])

        @pl.when(x + i_ref.shape[0] < split)
        def _():
            load(x + i_ref.shape[0]).start()

        return carry

    lax.fori_loop(0, total - split, kept, 0)
    lax.fori_loop(0, split, loaded, 0)
    for t in range(total - slots, total):
        save(t).wait()


def finish(me, near, far, saved, kept, ops):
    nx = saved.shape[0] + kept.shape[0]
    shape = (nx,) + saved.shape[1:]
    return pl.pallas_call(
        finish_kernel,
        in_specs=[SMEM] + [VMEM] * 8 + [HBM, VMEM, HBM, HBM],
        out_specs=HBM,
        out_shape=jax.ShapeDtypeStruct(shape, BF),
        scratch_shapes=[
            pltpu.VMEM((4, nx * 64, 128), F32),
            pltpu.VMEM((4, 32, NY, NZ), BF),
            pltpu.VMEM((4, 32, NY, NZ), BF),
            pltpu.VMEM((64, 256), BF),
            pltpu.VMEM((256, 64), BF),
            pltpu.VMEM((256, 1024), BF),
            pltpu.SemaphoreType.DMA((4,)),
            pltpu.SemaphoreType.DMA((4,)),
            pltpu.SemaphoreType.DMA((2,)),
        ],
        compiler_params=params(16),
        cost_estimate=cost(12),
        name="finish",
    )(
        me, *near, *far, in_hbm(saved), in_vmem(kept), in_hbm(ops["y"]), in_hbm(ops["z_back"])
    )


ACROSS = [(s, s ^ 4) for s in range(8)]
SWAP = [(0, 1), (1, 0)]


def in_square(blocks):
    return [blocks[0]] + [
        lax.ppermute(blocks[k], "space", [(s, s ^ k) for s in range(8)]) for k in (1, 2, 3)
    ]


def tuned_device(volume, cotangent, spectral_weight, pointwise_weight, gain_table, bias_index):
    ops = fixed_operands()
    nx = volume.shape[1]
    vol = volume.reshape(nx, 32, NY, NZ)
    cot = cotangent.reshape(nx, 32, NY, NZ)
    me = lax.axis_index("space").astype(jnp.int32).reshape(1)
    half = lax.axis_index("dp").astype(jnp.int32).reshape(1)
    weight = jnp.transpose(spectral_weight, (0, 1, 3, 4, 2))

    cot_blocks = lateral(me, cot, ops, me, "cotangent_lateral")
    cot_received = in_square(cot_blocks)
    vol_blocks = lateral(me, vol, ops, cot_blocks[0], "volume_lateral")
    cot_partner, passed = partner_modes(
        me, cot_received, ops, vol_blocks[1], "cotangent_partner"
    )
    other = lax.ppermute(cot_partner, "space", ACROSS)
    vol_received = in_square([vol_blocks[0], passed, vol_blocks[2], vol_blocks[3]])
    packed, kron = pack_weight(bias_index, weight, pointwise_weight, gain_table, cot_partner)
    g_modes, back_own = back_modes(me, cot_received, other, packed, ops)
    back_other = lax.ppermute(back_own, "space", ACROSS)
    vol_partner, _ = partner_modes(me, vol_received, ops, back_own, "volume_partner")
    vol_partner, *own_planes = back_planes(me, back_own, ops, vol_partner, "own_planes")
    back_near = in_square(own_planes)
    early = nx * 3 // 8
    saved, back_near[0] = pointwise(
        cot, kron, 0, early, own_planes[0], False, "pointwise_first"
    )
    vol_partner, *other_planes = back_planes(
        me, back_other, ops, vol_partner, "partner_planes", back_near[1:], [saved]
    )
    back_far = in_square(other_planes)
    kept, back_far[0] = pointwise(
        cot, kron, early, nx - early, other_planes[0], True, "pointwise_second"
    )
    vol_other = lax.ppermute(vol_partner, "space", ACROSS)
    out = finish(me, back_near, back_far, saved, kept, ops)
    u_modes = volume_modes(me, vol_received, vol_other, ops, [in_hbm(out)])
    g_other = lax.ppermute(g_modes, "dp", SWAP)
    u_other = lax.ppermute(u_modes, "dp", SWAP)
    grad = weight_grad(half, u_modes, u_other, g_modes, g_other)
    return out.reshape(volume.shape), jnp.transpose(grad, (0, 1, 4, 2, 3))


def per_device(volume, cotangent, spectral_weight, pointwise_weight, gain_table, bias_index):
    fits = (
        volume.shape == (1, 16, 32, NY, NZ)
        and spectral_weight.shape == (2, 2 * M, 64, 32, 32)
        and lax.axis_size("space") == 8
        and lax.axis_size("dp") == 2
    )
    device = tuned_device if fits else general_device
    return device(
        volume, cotangent, spectral_weight, pointwise_weight, gain_table, bias_index
    )


def solution(mesh):
    return jax.shard_map(
        per_device,
        mesh=mesh,
        in_specs=(
            P(("parts", "dp"), "space", None, None, None),
            P(("parts", "dp"), "space", None, None, None),
            P(None, None, "space", None, None),
            P(),
            P(),
            P(("parts", "dp")),
        ),
        out_specs=(
            P(("parts", "dp"), "space", None, None, None),
            P("parts", None, "space", None, "dp"),
        ),
        check_vma=False,
    )
```
